32 devices in a mesh: groups: 2 (over x), expert: 16 (over z, y, core).
Axes of the slice: x: 2, y: 2, z: 4, core: 2. Of those that a mesh axis runs over, the one named last changes fastest.
Arguments:
- hidden_in: bfloat16 [4096, 2048], P(('groups', 'expert')), parts along dimension 0, may hold values from -6 to 6
- norm_gain: float32 [2048], replicated, may hold values from 0.1 to 1.9
- router_weight: bfloat16 [2048, 16], replicated, may hold values from -0.125 to 0.125
- expert_ids: int32 [4096, 8], P(('groups', 'expert')), parts along dimension 0, may hold values from 0 to 15, all different within a row; in each aligned block of 128 rows (0 to 127, 128 to 255, ...) at most 96 rows name the same one
- w_gate: bfloat16 [16, 2048, 768], P('expert'), may hold values from -0.125 to 0.125
- w_up: bfloat16 [16, 2048, 768], P('expert'), may hold values from -0.125 to 0.125
- w_down: bfloat16 [16, 768, 2048], P('expert'), may hold values from -0.21875 to 0.21875
Outputs:
- combined: bfloat16 [4096, 2048], P(('groups', 'expert')), parts along dimension 0
The draws below stay inside these ranges and needn't reach their ends.
There are 2 independent parts, one for each index of `groups`. The reference program is written for one: setup_inputs(seed, part) draws one part's arguments, and reference() takes and returns one part's arrays. A program takes and returns all parts, laid end to end along the dimension named above; an argument that names none is the same for every part. Nothing has to cross between parts.
Inputs may be any that keep to these rules, and one draw needn't show every extreme that they name: `expert_ids`: each row names 8 different experts; within each aligned block of 128 rows (the rows of one device) no expert is named by more than 96 rows, a bound that some block reaches.
All inputs are finite; a program needn't handle non-finite values.
Results may differ from the reference program's by a relative error of at most 0.0074.
Values may be sent and summed in bfloat16 or wider, within the bound.
A program may use at most 128 MiB of HBM per device.

```python
import math
import jax
import jax.numpy as jnp
import numpy as np
from jax import lax

D = 2048
FF = 768
TOP = 8
TOK_DEV = 128
EXPERTS = 16
CAP = 96
TOKENS = 2048


def shard_levels(rng, shape, pieces, smallest, largest):
    gain = 1.0
    for axis_at, shards_of in pieces:
        heights = jax.random.uniform(jax.random.fold_in(jax.random.fold_in(rng, 6), axis_at), (shards_of,), jnp.float32, smallest / len(pieces), largest / len(pieces))
        gain = gain * jnp.repeat(jnp.exp(heights), shape[axis_at] // shards_of).reshape((-1,) + (1,) * (len(shape) - 1 - axis_at))
    return gain


def assign_block(own_key, own, number, rows, count, top, reach, skew):
    sequence = jax.random.permutation(own_key, count)
    crowded, common = shares(count, rows * top, reach, skew, True), shares(count, rows * top, reach, skew, False)
    places = jnp.arange(count)

    def named(lengths, offset_by):
        used = int((lengths > 0).sum())
        fixed = max(1, used // 4)
        passed = fixed + (places - fixed + offset_by * (used - fixed)) % max(1, count - fixed)
        return jnp.zeros((count,), jnp.int32).at[sequence[jnp.where(places < fixed, places, passed)]].set(jnp.asarray(lengths, jnp.int32))

    lengths = jnp.where(number % 4 == 0, named(crowded, number // 4), named(common, number - number // 4 - 1))
    mixed = jax.random.permutation(jax.random.fold_in(own, 3), count)
    donor, receiver = mixed[0:count // 2 * 2:2], mixed[1:count // 2 * 2:2]
    margin = jnp.minimum(lengths[donor] - 1, reach - lengths[receiver]) // 2
    margin = jnp.where((donor == sequence[0]) | (receiver == sequence[0]) | (lengths[receiver] == 0), 0, jnp.maximum(margin, 0))
    passed = jax.random.randint(jax.random.fold_in(own, 4), (count // 2,), 0, 1 << 20) % (margin + 1)
    lengths = lengths.at[donor].add(-passed).at[receiver].add(passed)
    items = jnp.searchsorted(jnp.cumsum(lengths), jnp.arange(rows * top), side="right").astype(jnp.int32)
    table = items.reshape(top, rows).T
    table = table[jax.random.permutation(jax.random.fold_in(own, 1), rows)]
    offset_by = jax.random.randint(jax.random.fold_in(own, 2), (rows, 1), 0, top)
    return jnp.take_along_axis(table, (jnp.arange(top)[None, :] + offset_by) % top, axis=1)


def shares(count, total, bound, slope, full):
    loads = [(1 << 20) // math.isqrt(grade ** slope) + 1 for grade in range(1, count + 1)]
    largest = bound if full else min(bound, max(-(-total // count), total * loads[0] // sum(loads)))
    least = 1 if total - largest >= count - 1 else 0
    holding, spare = [largest] + [least] * (count - 1), total - largest - least * (count - 1)
    while spare > 0:
        free = [i for i in range(1, count) if holding[i] < largest] or [i for i in range(1, count) if holding[i] < bound]
        mass, left = sum([loads[i] for i in free]), spare
        for i in free:
            more = min(bound - holding[i], max(1, left * loads[i] // mass), spare)
            holding[i] = holding[i] + more
            spare = spare - more
    return np.array(holding)


def normal_values(own_key, shape, spread, bound, split=(), held_as=jnp.bfloat16):
    values = spread * jax.random.normal(own_key, shape, jnp.float32)
    if split:
        values = values * shard_levels(own_key, shape, split, -0.22, 0.18)
    return jnp.clip(values, -bound, bound).astype(held_as)


def setup_inputs(seed: int = 0, part: int = 0) -> dict:
    key_of = jax.random.split(jax.random.key(seed), 8)
    part_splits = jax.random.split(jax.random.fold_in(key_of[7], part), 8)
    hidden_in = normal_values(part_splits[0], (TOKENS, D), 1.0, 6.0, ((0, 16),))
    norm_gain = jnp.clip(1.0 + 0.18 * jax.random.normal(key_of[1], (D,), jnp.float32), 0.1, 1.9)
    router_weight = normal_values(key_of[2], (D, EXPERTS), D ** -0.5, 0.125)
    expert_ids_keys = jax.random.split(jax.random.fold_in(part_splits[3], 1), TOKENS // TOK_DEV)
    expert_ids_turns = jax.random.permutation(jax.random.fold_in(part_splits[3], 3), TOKENS // TOK_DEV)
    expert_ids = jax.vmap(lambda own, number: assign_block(jax.random.fold_in(part_splits[3], 2), own, number, TOK_DEV, EXPERTS, TOP, CAP, 2))(expert_ids_keys, expert_ids_turns).reshape((TOKENS, TOP))
    w_gate = normal_values(key_of[4], (EXPERTS, D, FF), D ** -0.5, 0.125, ((0, 16),))
    w_up = normal_values(key_of[5], (EXPERTS, D, FF), D ** -0.5, 0.125, ((0, 16),))
    w_down = normal_values(key_of[6], (EXPERTS, FF, D), FF ** -0.5, 0.21875, ((0, 16),))
    return {"hidden_in": hidden_in, "norm_gain": norm_gain, "router_weight": router_weight, "expert_ids": expert_ids, "w_gate": w_gate, "w_up": w_up, "w_down": w_down}


def expert_mlp(item):
    rows, gate_w, up_w, down_w = item
    gate_act = jnp.dot(rows, gate_w, preferred_element_type=jnp.float32)
    up_act = jnp.dot(rows, up_w, preferred_element_type=jnp.float32)
    hidden = (jax.nn.silu(gate_act) * up_act).astype(jnp.bfloat16)
    return jnp.dot(hidden, down_w, preferred_element_type=jnp.float32).astype(jnp.bfloat16)

def reference(hidden_in, norm_gain, router_weight, expert_ids, w_gate, w_up, w_down):
    as_float = hidden_in.astype(jnp.float32)
    inv_rms = lax.rsqrt(lax.optimization_barrier(jnp.mean(as_float * as_float, axis=1, keepdims=True)) + 1e-06)
    normed = (as_float * inv_rms * norm_gain).astype(jnp.bfloat16)
    logits = jnp.dot(normed, router_weight, preferred_element_type=jnp.float32)
    exp_logits = jnp.exp(logits)
    picked = jnp.take_along_axis(exp_logits, expert_ids, axis=1)
    route_w = picked / lax.optimization_barrier(jnp.sum(picked, axis=1, keepdims=True))
    blocks = TOKENS // TOK_DEV
    flat_ids = expert_ids.reshape(blocks, TOK_DEV * TOP).astype(jnp.int32)
    onehot = (flat_ids[:, :, None] == jnp.arange(EXPERTS, dtype=jnp.int32)[None, None, :]).astype(jnp.int32)
    before = jnp.cumsum(onehot, axis=1) - onehot
    slot_index = lax.optimization_barrier(jnp.sum(before * onehot, axis=2)).astype(jnp.int32)
    block_index = jnp.arange(blocks, dtype=jnp.int32)[:, None]
    dest_index = (flat_ids * (blocks * CAP) + block_index * CAP + slot_index).reshape(-1).astype(jnp.int32)
    token_rows = jnp.repeat(normed, TOP, axis=0)
    packed = jnp.zeros((EXPERTS * blocks * CAP, D), jnp.bfloat16).at[dest_index].set(token_rows)
    packed = packed.reshape(EXPERTS, blocks * CAP, D)
    expert_out = lax.map(expert_mlp, (packed, w_gate, w_up, w_down)).reshape(EXPERTS * blocks * CAP, D)
    gathered = expert_out[dest_index].reshape(TOKENS, TOP, D)
    combined = lax.optimization_barrier(jnp.sum(gathered.astype(jnp.float32) * route_w[:, :, None], axis=1)).astype(jnp.bfloat16)
    return combined
```

```python
import jax
import jax.numpy as jnp
from jax import lax
from jax.experimental import pallas as pl
from jax.experimental.pallas import tpu as pltpu
from jax.sharding import PartitionSpec as P

DEPTH = 4
GRAIN = 16
GROUP = 4
INWARD, ACROSS, OUTWARD = range(3)
FORWARD, REDUCE, COMPUTE, ROUTE = range(4)

SPLIT = (2, 2, 2, 2)
ACROSS_LAST = (
    (True, True, False, False, False),
    (True, True, True, False, False),
)
STEPS = (
    (
        (0, 0, 0), (0, 2, 0), (3,), (0, 4, 0), (0, 3, 0), (0, 1, 0), (0, 0, 1), (0, 1, 2),
        (0, 4, 2), (2, 0, 0, 3, 0), (0, 2, 1), (2, 1, 2, 2, 0), (0, 3, 2), (0, 4, 1), (0, 2, 2), (0, 3, 1),
        (2, 0, 1, 2, 1), (2, 3, 2, 2, 2), (0, 4, 4), (0, 1, 1), (0, 0, 2), (0, 4, 3), (2, 3, 1, 1, 0), (1, 3, 2),
        (0, 1, 3), (0, 1, 4), (1, 0, 1), (2, 0, 2, 1, 1), (2, 1, 3, 1, 4), (0, 3, 4), (0, 3, 3), (0, 4, 5),
        (0, 0, 3), (1, 1, 1), (0, 2, 3), (1, 1, 3), (2, 3, 3, 3, 4), (2, 0, 3, 2, 3), (1, 3, 3), (0, 1, 5),
        (0, 2, 6), (0, 4, 6), (1, 3, 4), (0, 0, 6), (1, 0, 3), (1, 2, 3), (2, 2, 6, 1, 5), (0, 3, 6),
        (1, 2, 6), (1, 1, 2), (2, 3, 6, 0, 6), (0, 3, 5), (1, 1, 5), (0, 4, 7), (0, 0, 7), (1, 3, 6),
        (0, 1, 6), (2, 3, 5, 0, 7), (1, 0, 2), (0, 2, 7), (1, 0, 7), (1, 3, 5), (2, 1, 6, 2, 7), (0, 0, 4),
        (1, 2, 2), (1, 2, 7), (1, 1, 4), (0, 2, 4), (2, 2, 4, 0, 4), (0, 1, 7), (0, 3, 7), (1, 0, 6),
        (2, 3, 7, 1, 7), (0, 0, 5), (1, 1, 7), (1, 3, 7), (0, 2, 5), (2, 0, 5, 2, 5), (1, 1, 6), (1, 0, 5),
        (1, 2, 5), (1, 2, 1), (1, 0, 4), (1, 2, 4), (1, 0, 0), (1, 2, 0), (1, 3, 1), (1, 1, 0),
        (1, 3, 0),
    ),
    (
        (0, 1, 0), (3,), (0, 4, 0), (0, 3, 0), (0, 2, 0), (0, 0, 0), (0, 0, 6), (0, 1, 1),
        (0, 4, 2), (0, 4, 1), (0, 1, 2), (2, 1, 0, 0, 0), (0, 2, 6), (2, 1, 1, 3, 0), (0, 3, 2), (0, 4, 6),
        (2, 1, 2, 2, 0), (1, 1, 1), (0, 3, 6), (2, 3, 2, 2, 6), (0, 0, 1), (0, 3, 1), (0, 1, 6), (2, 3, 6, 0, 6),
        (0, 0, 7), (2, 3, 1, 0, 1), (0, 4, 7), (0, 2, 7), (0, 4, 3), (0, 1, 3), (0, 2, 4), (0, 4, 4),
        (0, 0, 4), (0, 2, 1), (1, 0, 1), (2, 2, 7, 1, 6), (0, 3, 4), (2, 2, 4, 1, 3), (0, 1, 7), (2, 0, 4, 2, 1),
        (1, 1, 3), (0, 3, 3), (2, 1, 7, 3, 4), (0, 4, 5), (1, 2, 1), (0, 0, 5), (0, 1, 4), (2, 3, 3, 0, 7),
        (1, 1, 7), (2, 1, 4, 0, 5), (1, 0, 7), (0, 2, 5), (1, 3, 2), (0, 0, 2), (0, 2, 2), (0, 3, 7),
        (1, 0, 5), (2, 0, 2, 2, 5), (1, 2, 4), (2, 2, 2, 3, 7), (0, 1, 5), (0, 3, 5), (2, 1, 5, 3, 5), (1, 2, 6),
        (1, 3, 4), (1, 1, 5), (0, 0, 3), (1, 3, 3), (1, 3, 6), (0, 2, 3), (2, 2, 3, 0, 3), (1, 3, 1),
        (1, 2, 5), (1, 0, 3), (1, 2, 3), (1, 1, 2), (1, 2, 7), (1, 3, 0), (1, 0, 4), (1, 1, 0),
        (1, 3, 5), (1, 0, 6), (1, 1, 4), (1, 3, 7), (1, 0, 2), (1, 1, 6), (1, 2, 2), (1, 0, 0),
        (1, 2, 0),
    ),
)

PARTS = len(SPLIT)
STARTS = tuple(sum(SPLIT[:part]) for part in range(PARTS))


def place_of(dz, dy):
    return dz % DEPTH * 2 + dy


def spot_of(kind, place):
    dz, dy = place // 2, place % 2
    return (dz - DEPTH if kind == 1 and dz == DEPTH - 1 else dz), dy


def along_z(kind):
    return {1: INWARD} if kind == 0 else {1: INWARD, -1: OUTWARD}


def across_last(kind, part, place):
    dz, _ = spot_of(kind, place)
    near = dz in (0, DEPTH - 1) if kind == 0 else dz in (0, 1)
    return ACROSS_LAST[kind if near else 1 - kind][part]


def onward(kind, part, place):
    dz, dy = spot_of(kind, place)
    links = along_z(kind)
    ways = (1, -1) if dz == 0 else ((-1,) if dz > 0 else (1,))
    depth_links = [links[way] for way in ways if way in links]
    if across_last(kind, part, place):
        return depth_links + [ACROSS] if dy == 0 else []
    return ([ACROSS] if dz == 0 and dy == 0 else []) + depth_links


def back(kind, part, place):
    dz, dy = spot_of(kind, place)
    if dy == 1 and (across_last(kind, part, place) or dz == 0):
        return ACROSS
    return along_z(kind)[1 if dz > 0 else -1]


def beyond(kind, link, place):
    dz, dy = spot_of(kind, place)
    if link == ACROSS:
        return kind, place_of(dz, 1 - dy), ACROSS
    if kind == 0:
        return 1, place_of(dz - 1, dy), OUTWARD
    if link == INWARD:
        return 1, place_of(1 - dz, dy), INWARD
    return 0, place_of(dz + 1, dy), INWARD


def grid_kernel(
    x_ref, gain_ref, router_ref, ids_ref, gate_hbm, up_hbm, down_hbm, out_ref,
    gate_w, up_w, down_w, xg, yb, ys, arrived, hb, routes, route_col, out_buf,
    load_sem, ag_s, ag_r, sx_s, sx_r, sy_s, sy_r, rs_s, rs_r, rt_s, rt_r, rx_s, rx_r, out_sem,
):
    rows, width = x_ref.shape
    me = lax.axis_index("expert")
    core = me % 2
    y_at = (me // 2) % 2
    z_at = me // 4
    is_corner = z_at % 3 == 0
    sibling = me + 1 - 2 * core

    def device_at(z, y):
        return (z * 2 + y) * 2 + core

    across = device_at(z_at, 1 - y_at)
    neighbours = (
        (device_at(1 + z_at // 3, y_at), across),
        (device_at(3 - z_at, y_at), across, device_at(3 * (z_at - 1), y_at)),
    )

    def by_kind(body):
        for kind in range(2):
            pl.when(is_corner if kind == 0 else jnp.logical_not(is_corner))(lambda kind=kind: body(kind))

    def greet(kind):
        for device in neighbours[kind] + (sibling,):
            pl.semaphore_signal(
                barrier, inc=1, device_id={"expert": device}, device_id_type=pl.DeviceIdType.MESH
            )

    def remote(src, dst, send, recv, device):
        return pltpu.make_async_remote_copy(
            src_ref=src, dst_ref=dst, send_sem=send, recv_sem=recv,
            device_id={"expert": device}, device_id_type=pl.DeviceIdType.MESH,
        )

    def grains(part, place):
        return pl.ds(place * (rows // GRAIN) + STARTS[part], SPLIT[part])

    def number(part, place):
        return place * PARTS + part

    def gather_copy(kind, link, part, place):
        _, there, _ = beyond(kind, link, place)
        return remote(
            xg.at[0, grains(part, place)], xg.at[0, grains(part, there)],
            ag_s.at[link, number(part, place)], ag_r.at[number(part, there)], neighbours[kind][link],
        )

    def gathered(part, place):
        at, slot = number(part, place), grains(part, place)
        return remote(xg.at[0, slot], xg.at[0, slot], ag_s.at[0, at], ag_r.at[at], sibling)

    def sibling_x(part, place):
        at, slot = number(part, place), grains(part, place)
        return remote(xg.at[0, slot], xg.at[1, slot], sx_s.at[at], sx_r.at[at], sibling)

    def sibling_y(part, place):
        at, slot = number(part, place), grains(part, place)
        return remote(yb.at[1, slot], ys.at[slot], sy_s.at[at], sy_r.at[at], sibling)

    def route_copy(kind, link, place):
        _, there, _ = beyond(kind, link, place)
        return remote(
            routes.at[0, place], routes.at[0, there], rt_s.at[link, place], rt_r.at[there],
            neighbours[kind][link],
        )

    def routed(place):
        return remote(routes.at[0, place], routes.at[0, place], rt_s.at[0, place], rt_r.at[place], sibling)

    def sibling_route(place):
        return remote(routes.at[0, place], routes.at[1, place], rx_s.at[place], rx_r.at[place], sibling)

    def reduce_copy(kind, part, place):
        link = back(kind, part, place)
        _, there, entry = beyond(kind, link, place)
        return remote(
            yb.at[0, grains(part, place)], arrived.at[entry, grains(part, there)],
            rs_s.at[number(part, place)], rs_r.at[entry, number(part, there)], neighbours[kind][link],
        )

    def reduced(link, part, place):
        at, slot = number(part, place), grains(part, place)
        return remote(yb.at[0, slot], arrived.at[link, slot], rs_s.at[at], rs_r.at[link, at], sibling)

    def out_copy(part):
        part_rows = pl.ds(STARTS[part] * GRAIN, SPLIT[part] * GRAIN)
        return pltpu.make_async_copy(out_buf.at[part_rows], out_ref.at[part_rows], out_sem.at[part])

    def forward(kind, part, place):
        if part == PARTS:
            if place != 0:
                routed(place).wait_recv()
            for link in onward(kind, part, place):
                route_copy(kind, link, place).start()
            sibling_route(place).start()
            return
        if place != 0:
            gathered(part, place).wait_recv()
        for link in onward(kind, part, place):
            gather_copy(kind, link, part, place).start()
        sibling_x(part, place).start()

    def reduce(kind, part, place):
        sibling_y(part, place).wait_recv()
        links = onward(kind, part, place)
        for link in links:
            reduced(link, part, place).wait_recv()
        for grain in range(SPLIT[part]):
            at = place * (rows // GRAIN) + STARTS[part] + grain
            value = yb[0, at].astype(jnp.float32) + ys[at].astype(jnp.float32)
            for link in links:
                value = value + arrived[link, at].astype(jnp.float32)
            value = value.astype(jnp.bfloat16)
            if place == 0:
                first = (STARTS[part] + grain) * GRAIN
                out_buf[first : first + GRAIN] = value
            else:
                yb[0, at] = value
        if place == 0:
            out_copy(part).start()
        else:
            reduce_copy(kind, part, place).start()

    diagonal = lax.broadcasted_iota(jnp.int32, (rows, rows), 0) == lax.broadcasted_iota(
        jnp.int32, (rows, rows), 1
    )

    def columns_of(place):
        sibling_route(place).wait_recv()
        for lane in range(2):
            values = routes[lane, place, pl.ds(me, 1), :]
            column = jnp.sum(jnp.where(diagonal, values, 0.0), axis=1, keepdims=True)
            spread = jnp.broadcast_to(column, (rows, rows))
            for grain in range(rows // GRAIN):
                at = place * (rows // GRAIN) + grain
                route_col[lane, at] = spread[grain * GRAIN : (grain + 1) * GRAIN]

    def route():
        logits = lax.dot_general(
            router_ref[...], xg[0, : rows // GRAIN].reshape(rows, width), (((1,), (1,)), ((), ())),
            preferred_element_type=jnp.float32,
        )
        exp_logits = jnp.exp(logits)
        expert_iota = lax.broadcasted_iota(jnp.int32, logits.shape, 0)
        chosen = expert_iota < 0
        for k in range(ids_ref.shape[0]):
            chosen = chosen | (ids_ref[k : k + 1, :] == expert_iota)
        picked = jnp.where(chosen, exp_logits, 0.0)
        routes[0, 0] = picked / jnp.sum(picked, axis=0, keepdims=True)

    def compute(corner_grains, middle_grains):
        at = [jnp.where(is_corner, a, b) for a, b in zip(corner_grains, middle_grains)]
        x = jnp.concatenate([xg[lane, a] for lane in range(2) for a in at], axis=0)
        gate = jnp.dot(x, gate_w[...], preferred_element_type=jnp.float32)
        up = jnp.dot(x, up_w[...], preferred_element_type=jnp.float32)
        hb[...] = (gate / (1.0 + jnp.exp(-gate)) * up).astype(jnp.bfloat16)
        y = jnp.dot(hb[...], down_w[...], preferred_element_type=jnp.float32)
        for lane in range(2):
            for i, a in enumerate(at):
                first = (lane * GROUP + i) * GRAIN
                weight = jnp.concatenate([route_col[lane, a]] * (width // rows), axis=1)
                yb[lane, a] = (y[first : first + GRAIN] * weight).astype(jnp.bfloat16)

    cuts = [[[]], [[]]]
    shared = [[], []]
    seen = [set(), set()]
    for kind in range(2):
        for step in STEPS[kind]:
            if step[0] == ROUTE:
                shared[kind].append(None)
                cuts[kind].append([])
            elif step[0] == COMPUTE:
                pieces = [(step[i], step[i + 1]) for i in range(1, len(step), 2)]
                for part, place in pieces:
                    cuts[kind][-1].append((sibling_x(part, place).wait_recv,))
                    if place not in seen[kind]:
                        seen[kind].add(place)
                        cuts[kind][-1].append((columns_of, place))
                shared[kind].append(
                    [place * (rows // GRAIN) + STARTS[part] + i for part, place in pieces for i in range(SPLIT[part])]
                )
                cuts[kind].append([(sibling_y(part, place).start,) for part, place in pieces])
            else:
                cuts[kind][-1].append((forward if step[0] == FORWARD else reduce, kind, step[1], step[2]))

    def section(index):
        def body(kind):
            for action, *details in cuts[kind][index]:
                action(*details)

        by_kind(body)

    def finish(kind):
        for place in range(2 * DEPTH):
            for part in range(PARTS):
                for link in onward(kind, part, place):
                    gather_copy(kind, link, part, place).wait_send()
                sibling_x(part, place).wait_send()
                sibling_y(part, place).wait_send()
                if place != 0:
                    reduce_copy(kind, part, place).wait_send()
            for link in onward(kind, PARTS, place):
                route_copy(kind, link, place).wait_send()
            sibling_route(place).wait_send()

    barrier = pltpu.get_barrier_semaphore()
    by_kind(greet)
    loads = [
        pltpu.make_async_copy(src.at[0], dst, load_sem.at[i])
        for i, (src, dst) in enumerate(((gate_hbm, gate_w), (up_hbm, up_w), (down_hbm, down_w)))
    ]
    for load in loads:
        load.start()
    as_float = x_ref[...].astype(jnp.float32)
    inv_rms = lax.rsqrt(jnp.mean(as_float * as_float, axis=1, keepdims=True) + 1e-06)
    normed = (as_float * inv_rms * gain_ref[...]).astype(jnp.bfloat16)
    xg[0, : rows // GRAIN] = normed.reshape(rows // GRAIN, GRAIN, width)
    by_kind(lambda kind: pl.semaphore_wait(barrier, len(neighbours[kind]) + 1))

    first = True
    for index, (corner, middle) in enumerate(zip(*shared)):
        section(index)
        if corner is None:
            route()
        else:
            if first:
                first = False
                for load in loads:
                    load.wait()
            compute(corner, middle)
    section(len(shared[0]))
    by_kind(finish)
    for part in range(PARTS):
        out_copy(part).wait()


def grid_local(hidden_in, norm_gain, router_weight, expert_ids, w_gate, w_up, w_down):
    rows, width = hidden_in.shape
    ff = w_gate.shape[2]
    count = router_weight.shape[1]
    places = 2 * DEPTH
    total = places * rows // GRAIN
    vmem = pl.BlockSpec(memory_space=pltpu.VMEM)
    hbm = pl.BlockSpec(memory_space=pl.ANY)
    dma = pltpu.SemaphoreType.DMA
    pieces = places * PARTS
    return pl.pallas_call(
        grid_kernel,
        out_shape=jax.ShapeDtypeStruct((rows, width), jnp.bfloat16),
        in_specs=[vmem, vmem, vmem, vmem, hbm, hbm, hbm],
        out_specs=hbm,
        scratch_shapes=[
            pltpu.VMEM((width, ff), jnp.bfloat16),
            pltpu.VMEM((width, ff), jnp.bfloat16),
            pltpu.VMEM((ff, width), jnp.bfloat16),
            pltpu.VMEM((2, total, GRAIN, width), jnp.bfloat16),
            pltpu.VMEM((2, total, GRAIN, width), jnp.bfloat16),
            pltpu.VMEM((total, GRAIN, width), jnp.bfloat16),
            pltpu.VMEM((3, total, GRAIN, width), jnp.bfloat16),
            pltpu.VMEM((2 * GROUP * GRAIN, ff), jnp.bfloat16),
            pltpu.VMEM((2, places, count, rows), jnp.float32),
            pltpu.VMEM((2, total, GRAIN, rows), jnp.float32),
            pltpu.VMEM((rows, width), jnp.bfloat16),
            dma((3,)), dma((3, pieces)), dma((pieces,)), dma((pieces,)), dma((pieces,)),
            dma((pieces,)), dma((pieces,)), dma((pieces,)), dma((3, pieces)),
            dma((3, places)), dma((places,)), dma((places,)), dma((places,)), dma((PARTS,)),
        ],
        compiler_params=pltpu.CompilerParams(
            collective_id=0, has_side_effects=True, vmem_limit_bytes=56 * 1024 * 1024
        ),
    )(hidden_in, norm_gain.reshape(1, width), router_weight.T, expert_ids.T, w_gate, w_up, w_down)


def local(hidden_in, norm_gain, router_weight, expert_ids, w_gate, w_up, w_down):
    tok_rows, width = hidden_in.shape
    top_count = expert_ids.shape[1]
    num_experts = router_weight.shape[1]
    dev_count = lax.axis_size("expert")
    local_experts = w_gate.shape[0]
    cap_rows = tok_rows * top_count * 3 // (2 * num_experts)
    as_float = hidden_in.astype(jnp.float32)
    inv_rms = lax.rsqrt(jnp.mean(as_float * as_float, axis=1, keepdims=True) + 1e-06)
    normed = (as_float * inv_rms * norm_gain).astype(jnp.bfloat16)
    logits = jnp.dot(normed, router_weight, preferred_element_type=jnp.float32)
    expert_iota = jnp.arange(num_experts, dtype=jnp.int32)
    chosen = jnp.any(expert_ids[:, :, None] == expert_iota[None, None, :], axis=1)
    picked = jnp.where(chosen, jnp.exp(logits), 0.0)
    route_w = picked / jnp.sum(picked, axis=1, keepdims=True)
    earlier = jnp.arange(tok_rows)[:, None] > jnp.arange(tok_rows)[None, :]
    slot_index = jnp.dot(
        earlier.astype(jnp.float32), chosen.astype(jnp.float32), precision=lax.Precision.HIGHEST
    ).astype(jnp.int32)
    dispatch = chosen[:, :, None] & (slot_index[:, :, None] == jnp.arange(cap_rows)[None, None, :])
    outgoing = jnp.einsum(
        "tes,td->esd", dispatch.astype(jnp.bfloat16), normed, preferred_element_type=jnp.float32
    ).astype(jnp.bfloat16)
    arrived = lax.all_to_all(
        outgoing.reshape(dev_count, local_experts, cap_rows, width), "expert", 0, 0, tiled=True
    )
    gate_act = jnp.einsum("semd,edf->semf", arrived, w_gate, preferred_element_type=jnp.float32)
    up_act = jnp.einsum("semd,edf->semf", arrived, w_up, preferred_element_type=jnp.float32)
    hidden = (jax.nn.silu(gate_act) * up_act).astype(jnp.bfloat16)
    expert_out = jnp.einsum("semf,efd->semd", hidden, w_down, preferred_element_type=jnp.float32)
    returned = lax.all_to_all(expert_out.astype(jnp.bfloat16), "expert", 0, 0, tiled=True)
    combined = jnp.einsum(
        "tes,esd->td",
        jnp.where(dispatch, route_w[:, :, None], 0.0),
        returned.reshape(num_experts, cap_rows, width).astype(jnp.float32),
        precision=lax.Precision.HIGHEST,
    )
    return combined.astype(jnp.bfloat16)


def solution(mesh):
    in_specs = (
        P(("groups", "expert"), None),
        P(),
        P(),
        P(("groups", "expert"), None),
        P("expert", None, None),
        P("expert", None, None),
        P("expert", None, None),
    )
    out_specs = P(("groups", "expert"), None)
    gridded = mesh.shape["expert"] == 4 * DEPTH
    body = grid_local if gridded else local
    return jax.shard_map(body, mesh=mesh, in_specs=in_specs, out_specs=out_specs, check_vma=False)
```

```python
import jax
import jax.numpy as jnp
from jax import lax
from jax.experimental import pallas as pl
from jax.experimental.pallas import tpu as pltpu
from jax.sharding import PartitionSpec as P

DEPTH = 4
GRAIN = 16
GROUP = 4
INWARD, ACROSS, OUTWARD = range(3)
FORWARD, REDUCE, COMPUTE, ROUTE = range(4)

SPLIT = (2, 2, 1, 1, 1, 1)
ACROSS_LAST = (
    (True, True, False, False, False, False, False),
    (True, True, True, False, False, False, False),
)
STEPS = (
    (
        (0, 5, 0), (0, 4, 0), (3,), (0, 1, 0), (0, 6, 0), (0, 0, 0), (0, 2, 0), (0, 3, 0),
        (0, 5, 2), (0, 5, 1), (0, 6, 2), (0, 4, 1), (2, 0, 0, 3, 0, 5, 2), (0, 1, 1), (0, 6, 1), (0, 2, 2),
        (0, 0, 2), (1, 5, 2), (2, 2, 0, 5, 1, 4, 0, 4, 1), (0, 4, 2), (2, 0, 2, 5, 0, 2, 2), (0, 0, 1), (0, 2, 1), (0, 3, 2),
        (0, 3, 1), (0, 1, 2), (2, 2, 1, 0, 1, 4, 2), (2, 3, 2, 3, 1, 1, 2), (1, 0, 1), (0, 5, 3), (0, 5, 4), (0, 6, 4),
        (1, 4, 2), (0, 0, 3), (0, 6, 3), (0, 2, 3), (1, 3, 2), (2, 0, 3, 5, 4, 5, 3), (0, 4, 4), (0, 1, 3),
        (0, 0, 4), (0, 3, 4), (1, 0, 3), (1, 5, 3), (2, 0, 4, 4, 4, 2, 3), (0, 4, 3), (1, 5, 4), (0, 4, 6),
        (1, 4, 4), (2, 4, 3, 3, 4, 1, 3), (0, 5, 5), (0, 0, 5), (1, 2, 3), (1, 3, 4), (1, 1, 3), (1, 0, 2),
        (0, 2, 6), (1, 4, 3), (0, 6, 6), (2, 1, 0, 1, 1), (0, 1, 6), (1, 2, 2), (0, 6, 5), (1, 1, 1),
        (2, 2, 6, 1, 6, 4, 6), (0, 3, 6), (1, 1, 2), (0, 0, 6), (1, 4, 6), (2, 5, 5, 3, 6, 0, 5), (0, 1, 7), (0, 4, 5),
        (1, 2, 6), (1, 3, 6), (0, 4, 7), (1, 0, 5), (0, 6, 7), (1, 5, 5), (0, 3, 7), (2, 4, 7, 0, 6, 4, 5),
        (0, 2, 7), (0, 0, 7), (1, 4, 7), (2, 1, 7, 3, 7, 2, 7), (0, 1, 4), (1, 4, 5), (1, 0, 4), (1, 1, 7),
        (2, 0, 7, 1, 4), (1, 2, 7), (0, 2, 4), (0, 5, 6), (0, 5, 7), (1, 0, 7), (0, 1, 5), (1, 3, 7),
        (0, 3, 3), (2, 5, 7, 2, 4, 1, 5), (1, 1, 6), (1, 5, 7), (1, 1, 5), (0, 2, 5), (0, 3, 5), (1, 0, 6),
        (2, 3, 3, 2, 5, 3, 5, 5, 6), (1, 4, 1), (1, 5, 6), (1, 2, 5), (1, 3, 5), (1, 3, 1), (1, 1, 4), (1, 3, 3),
        (1, 4, 0), (1, 2, 1), (1, 2, 4), (1, 3, 0), (1, 2, 0), (1, 1, 0), (1, 5, 1), (1, 0, 0),
        (1, 5, 0),
    ),
    (
        (0, 5, 0), (3,), (0, 6, 0), (0, 0, 0), (0, 2, 0), (0, 4, 0), (0, 3, 0), (0, 1, 0),
        (0, 5, 1), (0, 6, 2), (0, 6, 1), (0, 5, 2), (0, 5, 6), (0, 4, 6), (2, 3, 0, 1, 0, 5, 2), (0, 1, 6),
        (0, 0, 2), (0, 6, 6), (0, 2, 1), (0, 0, 1), (2, 4, 0, 5, 1, 0, 0), (2, 4, 6, 0, 1, 2, 0), (0, 2, 6), (0, 4, 2),
        (0, 0, 6), (0, 3, 2), (0, 1, 1), (0, 3, 6), (0, 4, 1), (2, 0, 6, 5, 6, 4, 2), (2, 4, 1, 3, 6, 1, 1), (0, 6, 3),
        (0, 1, 7), (0, 4, 4), (0, 5, 3), (0, 4, 7), (1, 0, 1), (0, 6, 7), (0, 0, 3), (0, 2, 7),
        (2, 5, 3, 2, 6, 0, 2), (2, 4, 7, 2, 7, 1, 7), (0, 2, 4), (0, 3, 7), (0, 6, 4), (0, 1, 4), (1, 1, 7), (0, 0, 7),
        (2, 2, 4, 4, 4, 0, 3), (0, 3, 4), (0, 0, 4), (2, 0, 7, 3, 7, 2, 1), (1, 0, 3), (0, 4, 3), (1, 5, 2), (0, 6, 5),
        (1, 4, 2), (2, 4, 3, 3, 4, 1, 4), (0, 4, 5), (0, 1, 5), (0, 3, 5), (0, 2, 5), (1, 0, 7), (2, 4, 5, 1, 6, 3, 2),
        (2, 1, 5, 2, 5, 3, 5), (1, 3, 2), (0, 5, 7), (1, 2, 1), (0, 0, 5), (0, 1, 2), (2, 5, 7, 0, 4, 5, 0), (2, 1, 2, 0, 5),
        (1, 4, 4), (0, 5, 5), (1, 1, 1), (1, 0, 5), (1, 2, 4), (0, 2, 2), (1, 1, 5), (0, 1, 3),
        (0, 5, 4), (1, 3, 4), (0, 3, 1), (1, 4, 6), (2, 1, 3, 5, 4, 5, 5), (1, 2, 6), (1, 5, 3), (1, 3, 6),
        (1, 1, 3), (1, 4, 5), (1, 4, 3), (0, 3, 3), (1, 5, 1), (0, 2, 3), (1, 0, 2), (1, 4, 7),
        (2, 2, 3, 3, 3, 2, 2, 3, 1), (1, 4, 1), (1, 3, 5), (1, 2, 5), (1, 2, 3), (1, 0, 0), (1, 1, 4), (1, 3, 7),
        (1, 5, 0), (1, 5, 5), (1, 2, 7), (1, 4, 0), (1, 0, 4), (1, 1, 6), (1, 5, 4), (1, 5, 7),
        (1, 3, 3), (1, 0, 6), (1, 1, 2), (1, 5, 6), (1, 3, 1), (1, 2, 2), (1, 3, 0), (1, 1, 0),
        (1, 2, 0),
    ),
)

PARTS = len(SPLIT)
STARTS = tuple(sum(SPLIT[:part]) for part in range(PARTS))


def place_of(dz, dy):
    return dz % DEPTH * 2 + dy


def spot_of(kind, place):
    dz, dy = place // 2, place % 2
    return (dz - DEPTH if kind == 1 and dz == DEPTH - 1 else dz), dy


def along_z(kind):
    return {1: INWARD} if kind == 0 else {1: INWARD, -1: OUTWARD}


def across_last(kind, part, place):
    dz, _ = spot_of(kind, place)
    near = dz in (0, DEPTH - 1) if kind == 0 else dz in (0, 1)
    return ACROSS_LAST[kind if near else 1 - kind][part]


def onward(kind, part, place):
    dz, dy = spot_of(kind, place)
    links = along_z(kind)
    ways = (1, -1) if dz == 0 else ((-1,) if dz > 0 else (1,))
    depth_links = [links[way] for way in ways if way in links]
    if across_last(kind, part, place):
        return depth_links + [ACROSS] if dy == 0 else []
    return ([ACROSS] if dz == 0 and dy == 0 else []) + depth_links


def back(kind, part, place):
    dz, dy = spot_of(kind, place)
    if dy == 1 and (across_last(kind, part, place) or dz == 0):
        return ACROSS
    return along_z(kind)[1 if dz > 0 else -1]


def beyond(kind, link, place):
    dz, dy = spot_of(kind, place)
    if link == ACROSS:
        return kind, place_of(dz, 1 - dy), ACROSS
    if kind == 0:
        return 1, place_of(dz - 1, dy), OUTWARD
    if link == INWARD:
        return 1, place_of(1 - dz, dy), INWARD
    return 0, place_of(dz + 1, dy), INWARD


def grid_kernel(
    x_hbm, gain_hbm, router_hbm, ids_hbm, gate_hbm, up_hbm, down_hbm, out_ref,
    x_ref, gain_ref, router_ref, ids_ref, gate_w, up_w, down_w, xg, yb, ys, arrived, hb, routes, route_col, out_buf,
    in_sem, load_sem, ag_s, ag_r, sx_s, sx_r, sy_s, sy_r, rs_s, rs_r, rt_s, rt_r, rx_s, rx_r, out_sem,
):
    rows, width = x_ref.shape
    me = lax.axis_index("expert")
    core = me % 2
    y_at = (me // 2) % 2
    z_at = me // 4
    is_corner = z_at % 3 == 0
    sibling = me + 1 - 2 * core

    def device_at(z, y):
        return (z * 2 + y) * 2 + core

    across = device_at(z_at, 1 - y_at)
    neighbours = (
        (device_at(1 + z_at // 3, y_at), across),
        (device_at(3 - z_at, y_at), across, device_at(3 * (z_at - 1), y_at)),
    )

    def by_kind(body):
        for kind in range(2):
            pl.when(is_corner if kind == 0 else jnp.logical_not(is_corner))(lambda kind=kind: body(kind))

    def greet(kind):
        for device in neighbours[kind] + (sibling,):
            pl.semaphore_signal(
                barrier, inc=1, device_id={"expert": device}, device_id_type=pl.DeviceIdType.MESH
            )

    def remote(src, dst, send, recv, device):
        return pltpu.make_async_remote_copy(
            src_ref=src, dst_ref=dst, send_sem=send, recv_sem=recv,
            device_id={"expert": device}, device_id_type=pl.DeviceIdType.MESH,
        )

    def grains(part, place):
        return pl.ds(place * (rows // GRAIN) + STARTS[part], SPLIT[part])

    def number(part, place):
        return place * PARTS + part

    def gather_copy(kind, link, part, place):
        _, there, _ = beyond(kind, link, place)
        return remote(
            xg.at[0, grains(part, place)], xg.at[0, grains(part, there)],
            ag_s.at[link], ag_r.at[number(part, there)], neighbours[kind][link],
        )

    def gathered(part, place):
        at, slot = number(part, place), grains(part, place)
        return remote(xg.at[0, slot], xg.at[0, slot], ag_s.at[0], ag_r.at[at], sibling)

    def sibling_x(part, place):
        at, slot = number(part, place), grains(part, place)
        return remote(xg.at[0, slot], xg.at[1, slot], sx_s.at[0], sx_r.at[at], sibling)

    def sibling_y(part, place):
        at, slot = number(part, place), grains(part, place)
        return remote(yb.at[1, slot], ys.at[slot], sy_s.at[0], sy_r.at[at], sibling)

    def route_copy(kind, link, place):
        _, there, _ = beyond(kind, link, place)
        return remote(
            routes.at[0, place], routes.at[0, there], rt_s.at[link], rt_r.at[there],
            neighbours[kind][link],
        )

    def routed(place):
        return remote(routes.at[0, place], routes.at[0, place], rt_s.at[0], rt_r.at[place], sibling)

    def sibling_route(place):
        return remote(routes.at[0, place], routes.at[1, place], rx_s.at[0], rx_r.at[place], sibling)

    def reduce_copy(kind, part, place):
        link = back(kind, part, place)
        _, there, entry = beyond(kind, link, place)
        return remote(
            yb.at[0, grains(part, place)], arrived.at[entry, grains(part, there)],
            rs_s.at[0], rs_r.at[entry, number(part, there)], neighbours[kind][link],
        )

    def reduced(link, part, place):
        at, slot = number(part, place), grains(part, place)
        return remote(yb.at[0, slot], arrived.at[link, slot], rs_s.at[0], rs_r.at[link, at], sibling)

    def out_copy(part):
        part_rows = pl.ds(STARTS[part] * GRAIN, SPLIT[part] * GRAIN)
        return pltpu.make_async_copy(out_buf.at[part_rows], out_ref.at[part_rows], out_sem.at[part])

    def in_copy(part):
        part_rows = pl.ds(STARTS[part] * GRAIN, SPLIT[part] * GRAIN)
        return pltpu.make_async_copy(x_hbm.at[part_rows], x_ref.at[part_rows], in_sem.at[part])

    def norm(part):
        in_copy(part).wait()
        first, last = STARTS[part], STARTS[part] + SPLIT[part]
        as_float = x_ref[first * GRAIN : last * GRAIN].astype(jnp.float32)
        inv_rms = lax.rsqrt(jnp.mean(as_float * as_float, axis=1, keepdims=True) + 1e-06)
        normed = (as_float * inv_rms * gain_ref[...]).astype(jnp.bfloat16)
        xg[0, first:last] = normed.reshape(last - first, GRAIN, width)

    def forward(kind, part, place):
        if part == PARTS:
            if place != 0:
                routed(place).wait_recv()
            for link in onward(kind, part, place):
                route_copy(kind, link, place).start()
            sibling_route(place).start()
            return
        if place != 0:
            gathered(part, place).wait_recv()
        for link in onward(kind, part, place):
            gather_copy(kind, link, part, place).start()
        sibling_x(part, place).start()

    def reduce(kind, part, place):
        sibling_y(part, place).wait_recv()
        links = onward(kind, part, place)
        for link in links:
            reduced(link, part, place).wait_recv()
        for grain in range(SPLIT[part]):
            at = place * (rows // GRAIN) + STARTS[part] + grain
            value = yb[0, at].astype(jnp.float32) + ys[at].astype(jnp.float32)
            for link in links:
                value = value + arrived[link, at].astype(jnp.float32)
            value = value.astype(jnp.bfloat16)
            if place == 0:
                first = (STARTS[part] + grain) * GRAIN
                out_buf[first : first + GRAIN] = value
            else:
                yb[0, at] = value
        if place == 0:
            out_copy(part).start()
        else:
            reduce_copy(kind, part, place).start()

    diagonal = lax.broadcasted_iota(jnp.int32, (rows, rows), 0) == lax.broadcasted_iota(
        jnp.int32, (rows, rows), 1
    )

    def columns_of(place):
        sibling_route(place).wait_recv()
        for lane in range(2):
            values = routes[lane, place, pl.ds(me, 1), :]
            column = jnp.sum(jnp.where(diagonal, values, 0.0), axis=1, keepdims=True)
            spread = jnp.broadcast_to(column, (rows, rows))
            for grain in range(rows // GRAIN):
                at = place * (rows // GRAIN) + grain
                route_col[lane, at] = spread[grain * GRAIN : (grain + 1) * GRAIN]

    def route():
        logits = lax.dot_general(
            router_ref[...], xg[0, : rows // GRAIN].reshape(rows, width), (((1,), (1,)), ((), ())),
            preferred_element_type=jnp.float32,
        )
        exp_logits = jnp.exp(logits)
        expert_iota = lax.broadcasted_iota(jnp.int32, logits.shape, 0)
        chosen = expert_iota < 0
        for k in range(ids_ref.shape[0]):
            chosen = chosen | (ids_ref[k : k + 1, :] == expert_iota)
        picked = jnp.where(chosen, exp_logits, 0.0)
        routes[0, 0] = picked / jnp.sum(picked, axis=0, keepdims=True)

    def compute(corner_grains, middle_grains):
        at = [jnp.where(is_corner, a, b) for a, b in zip(corner_grains, middle_grains)]
        x = jnp.concatenate([xg[lane, a] for lane in range(2) for a in at], axis=0)
        gate = jnp.dot(x, gate_w[...], preferred_element_type=jnp.float32)
        up = jnp.dot(x, up_w[...], preferred_element_type=jnp.float32)
        hb[...] = (gate / (1.0 + jnp.exp(-gate)) * up).astype(jnp.bfloat16)
        y = jnp.dot(hb[...], down_w[...], preferred_element_type=jnp.float32)
        for lane in range(2):
            for i, a in enumerate(at):
                first = (lane * GROUP + i) * GRAIN
                weight = jnp.concatenate([route_col[lane, a]] * (width // rows), axis=1)
                yb[lane, a] = (y[first : first + GRAIN] * weight).astype(jnp.bfloat16)

    cuts = [[[]], [[]]]
    shared = [[], []]
    seen = [set(), set()]
    for kind in range(2):
        for step in STEPS[kind]:
            if step[0] == ROUTE:
                shared[kind].append(None)
                cuts[kind].append([])
            elif step[0] == COMPUTE:
                pieces = [(step[i], step[i + 1]) for i in range(1, len(step), 2)]
                for part, place in pieces:
                    cuts[kind][-1].append((sibling_x(part, place).wait_recv,))
                    if place not in seen[kind]:
                        seen[kind].add(place)
                        cuts[kind][-1].append((columns_of, place))
                shared[kind].append(
                    [place * (rows // GRAIN) + STARTS[part] + i for part, place in pieces for i in range(SPLIT[part])]
                )
                cuts[kind].append([(sibling_y(part, place).start,) for part, place in pieces])
            else:
                cuts[kind][-1].append((forward if step[0] == FORWARD else reduce, kind, step[1], step[2]))

    def section(index):
        def body(kind):
            for action, *details in cuts[kind][index]:
                action(*details)

        by_kind(body)

    def finish(kind):
        for link, device in enumerate(neighbours[kind]):
            sent = sum(
                SPLIT[part]
                for place in range(2 * DEPTH)
                for part in range(PARTS)
                if link in onward(kind, part, place)
            )
            slot = xg.at[0, pl.ds(0, sent)]
            remote(slot, slot, ag_s.at[link], ag_r.at[0], device).wait_send()
            sent = sum(link in onward(kind, PARTS, place) for place in range(2 * DEPTH))
            if sent:
                slot = routes.at[0, pl.ds(0, sent)]
                remote(slot, slot, rt_s.at[link], rt_r.at[0], device).wait_send()
        remote(xg.at[0], xg.at[1], sx_s.at[0], sx_r.at[0], sibling).wait_send()
        remote(yb.at[1], ys, sy_s.at[0], sy_r.at[0], sibling).wait_send()
        remote(routes.at[0], routes.at[1], rx_s.at[0], rx_r.at[0], sibling).wait_send()
        returned = pl.ds(rows // GRAIN, (2 * DEPTH - 1) * (rows // GRAIN))
        remote(yb.at[0, returned], ys.at[returned], rs_s.at[0], rs_r.at[0, 0], sibling).wait_send()

    barrier = pltpu.get_barrier_semaphore()
    by_kind(greet)
    small = [
        pltpu.make_async_copy(src, dst, in_sem.at[PARTS + i])
        for i, (src, dst) in enumerate(((gain_hbm, gain_ref), (router_hbm, router_ref), (ids_hbm, ids_ref)))
    ]
    small[0].start()
    for part in range(PARTS):
        in_copy(part).start()
    for copy in small[1:]:
        copy.start()
    loads = [
        pltpu.make_async_copy(src.at[0], dst, load_sem.at[i])
        for i, (src, dst) in enumerate(((gate_hbm, gate_w), (up_hbm, up_w), (down_hbm, down_w)))
    ]
    for load in loads:
        load.start()
    small[0].wait()
    for kind in range(2):
        opening, waits = [], [(pl.semaphore_wait, barrier, len(neighbours[kind]) + 1)]
        for entry in cuts[kind][0]:
            if entry[0] is forward and entry[3] == 0:
                opening.append((norm, entry[2]))
            opening += waits
            waits = []
            opening.append(entry)
        done = [entry[1] for entry in opening if entry[0] is norm]
        opening += [(norm, part) for part in range(PARTS) if part not in done]
        cuts[kind][0] = opening

    first = True
    for index, (corner, middle) in enumerate(zip(*shared)):
        section(index)
        if corner is None:
            for copy in small[1:]:
                copy.wait()
            route()
        else:
            if first:
                first = False
                for load in loads:
                    load.wait()
            compute(corner, middle)
    section(len(shared[0]))
    by_kind(finish)
    for part in range(PARTS):
        out_copy(part).wait()


def grid_local(hidden_in, norm_gain, router_weight, expert_ids, w_gate, w_up, w_down):
    rows, width = hidden_in.shape
    ff = w_gate.shape[2]
    count = router_weight.shape[1]
    places = 2 * DEPTH
    total = places * rows // GRAIN
    hbm = pl.BlockSpec(memory_space=pl.ANY)
    dma = pltpu.SemaphoreType.DMA
    pieces = places * PARTS
    return pl.pallas_call(
        grid_kernel,
        out_shape=jax.ShapeDtypeStruct((rows, width), jnp.bfloat16),
        in_specs=[hbm] * 7,
        out_specs=hbm,
        scratch_shapes=[
            pltpu.VMEM((rows, width), jnp.bfloat16),
            pltpu.VMEM((1, width), jnp.float32),
            pltpu.VMEM((count, width), jnp.bfloat16),
            pltpu.VMEM(expert_ids.shape[::-1], jnp.int32),
            pltpu.VMEM((width, ff), jnp.bfloat16),
            pltpu.VMEM((width, ff), jnp.bfloat16),
            pltpu.VMEM((ff, width), jnp.bfloat16),
            pltpu.VMEM((2, total, GRAIN, width), jnp.bfloat16),
            pltpu.VMEM((2, total, GRAIN, width), jnp.bfloat16),
            pltpu.VMEM((total, GRAIN, width), jnp.bfloat16),
            pltpu.VMEM((3, total, GRAIN, width), jnp.bfloat16),
            pltpu.VMEM((2 * GROUP * GRAIN, ff), jnp.bfloat16),
            pltpu.VMEM((2, places, count, rows), jnp.float32),
            pltpu.VMEM((2, total, GRAIN, rows), jnp.float32),
            pltpu.VMEM((rows, width), jnp.bfloat16),
            dma((PARTS + 3,)), dma((3,)), dma((3,)), dma((pieces,)), dma((1,)), dma((pieces,)),
            dma((1,)), dma((pieces,)), dma((1,)), dma((3, pieces)),
            dma((3,)), dma((places,)), dma((1,)), dma((places,)), dma((PARTS,)),
        ],
        compiler_params=pltpu.CompilerParams(
            collective_id=0, has_side_effects=True, vmem_limit_bytes=56 * 1024 * 1024
        ),
    )(hidden_in, norm_gain.reshape(1, width), router_weight.T, expert_ids.T, w_gate, w_up, w_down)


def local(hidden_in, norm_gain, router_weight, expert_ids, w_gate, w_up, w_down):
    tok_rows, width = hidden_in.shape
    top_count = expert_ids.shape[1]
    num_experts = router_weight.shape[1]
    dev_count = lax.axis_size("expert")
    local_experts = w_gate.shape[0]
    cap_rows = tok_rows * top_count * 3 // (2 * num_experts)
    as_float = hidden_in.astype(jnp.float32)
    inv_rms = lax.rsqrt(jnp.mean(as_float * as_float, axis=1, keepdims=True) + 1e-06)
    normed = (as_float * inv_rms * norm_gain).astype(jnp.bfloat16)
    logits = jnp.dot(normed, router_weight, preferred_element_type=jnp.float32)
    expert_iota = jnp.arange(num_experts, dtype=jnp.int32)
    chosen = jnp.any(expert_ids[:, :, None] == expert_iota[None, None, :], axis=1)
    picked = jnp.where(chosen, jnp.exp(logits), 0.0)
    route_w = picked / jnp.sum(picked, axis=1, keepdims=True)
    earlier = jnp.arange(tok_rows)[:, None] > jnp.arange(tok_rows)[None, :]
    slot_index = jnp.dot(
        earlier.astype(jnp.float32), chosen.astype(jnp.float32), precision=lax.Precision.HIGHEST
    ).astype(jnp.int32)
    dispatch = chosen[:, :, None] & (slot_index[:, :, None] == jnp.arange(cap_rows)[None, None, :])
    outgoing = jnp.einsum(
        "tes,td->esd", dispatch.astype(jnp.bfloat16), normed, preferred_element_type=jnp.float32
    ).astype(jnp.bfloat16)
    arrived = lax.all_to_all(
        outgoing.reshape(dev_count, local_experts, cap_rows, width), "expert", 0, 0, tiled=True
    )
    gate_act = jnp.einsum("semd,edf->semf", arrived, w_gate, preferred_element_type=jnp.float32)
    up_act = jnp.einsum("semd,edf->semf", arrived, w_up, preferred_element_type=jnp.float32)
    hidden = (jax.nn.silu(gate_act) * up_act).astype(jnp.bfloat16)
    expert_out = jnp.einsum("semf,efd->semd", hidden, w_down, preferred_element_type=jnp.float32)
    returned = lax.all_to_all(expert_out.astype(jnp.bfloat16), "expert", 0, 0, tiled=True)
    combined = jnp.einsum(
        "tes,esd->td",
        jnp.where(dispatch, route_w[:, :, None], 0.0),
        returned.reshape(num_experts, cap_rows, width).astype(jnp.float32),
        precision=lax.Precision.HIGHEST,
    )
    return combined.astype(jnp.bfloat16)


def solution(mesh):
    in_specs = (
        P(("groups", "expert"), None),
        P(),
        P(),
        P(("groups", "expert"), None),
        P("expert", None, None),
        P("expert", None, None),
        P("expert", None, None),
    )
    out_specs = P(("groups", "expert"), None)
    gridded = mesh.shape["expert"] == 4 * DEPTH
    body = grid_local if gridded else local
    return jax.shard_map(body, mesh=mesh, in_specs=in_specs, out_specs=out_specs, check_vma=False)
```

```python
import jax
import jax.numpy as jnp
from jax import lax
from jax.experimental import pallas as pl
from jax.experimental.pallas import tpu as pltpu
from jax.sharding import PartitionSpec as P

DEPTH = 4
GRAIN = 16
GROUP = 4
INWARD, ACROSS, OUTWARD = range(3)
ARRIVE, REDUCE, COMPUTE, ROUTE, SEND = range(5)

SPLIT = (2, 2, 2, 2)
ACROSS_LAST = (
    (True, True, False, False, False),
    (True, True, True, False, False),
)
STEPS = (
    (
        (0, 0, 0), (4, 1, 0, 0), (0, 1, 0), (4, 1, 1, 0), (3,), (0, 4, 0), (4, 0, 0, 0), (0, 2, 0),
        (4, 0, 2, 0), (0, 3, 0), (4, 1, 3, 0), (2, 2, 0, 0, 0), (4, 1, 2, 0), (2, 1, 0, 3, 0), (0, 4, 1), (0, 1, 1),
        (0, 1, 2), (0, 0, 1), (0, 3, 2), (4, 0, 3, 0), (4, 1, 1, 2), (4, 0, 1, 0), (0, 4, 2), (2, 0, 1, 1, 1),
        (2, 1, 2, 3, 2), (1, 1, 1), (0, 4, 3), (0, 0, 2), (0, 2, 1), (4, 0, 2, 1), (0, 3, 3), (0, 4, 4),
        (1, 0, 1), (1, 3, 2), (2, 0, 2, 2, 1), (0, 1, 3), (0, 3, 1), (4, 0, 3, 1), (0, 1, 4), (0, 4, 5),
        (4, 1, 1, 4), (0, 4, 6), (2, 1, 3, 3, 3), (2, 3, 1, 1, 4), (0, 4, 7), (0, 0, 6), (4, 1, 0, 6), (1, 3, 3),
        (1, 1, 3), (0, 3, 4), (0, 1, 5), (2, 0, 6, 3, 4), (0, 3, 5), (4, 1, 0, 2), (0, 0, 7), (1, 3, 4),
        (2, 1, 5, 3, 5), (0, 2, 6), (1, 1, 2), (1, 1, 5), (2, 0, 7, 2, 6), (0, 1, 6), (1, 3, 5), (0, 0, 3),
        (4, 1, 1, 6), (1, 2, 6), (1, 0, 7), (2, 0, 3, 1, 6), (0, 2, 4), (1, 1, 4), (1, 0, 3), (0, 0, 4),
        (0, 1, 7), (2, 2, 4, 0, 4), (4, 1, 0, 4), (0, 3, 6), (1, 0, 6), (2, 3, 6, 1, 7), (0, 2, 2), (4, 1, 2, 2),
        (1, 3, 6), (1, 0, 2), (4, 1, 2, 4), (0, 2, 7), (0, 0, 5), (2, 2, 7, 2, 2), (1, 1, 7), (0, 3, 7),
        (1, 2, 7), (0, 2, 3), (2, 0, 5, 3, 7), (1, 3, 7), (0, 2, 5), (1, 0, 5), (2, 2, 5, 2, 3), (1, 1, 6),
        (1, 0, 0), (1, 2, 5), (1, 2, 3), (1, 0, 4), (1, 2, 4), (1, 2, 1), (1, 2, 2), (1, 3, 1),
        (1, 2, 0), (1, 1, 0), (1, 3, 0),
    ),
    (
        (0, 2, 0), (4, 0, 2, 0), (0, 3, 0), (4, 2, 3, 0), (3,), (0, 4, 0), (4, 0, 3, 0), (4, 1, 3, 0),
        (0, 1, 0), (4, 2, 1, 0), (4, 1, 1, 0), (0, 0, 0), (4, 0, 1, 0), (4, 2, 0, 0), (0, 4, 1), (0, 4, 6),
        (2, 3, 0, 2, 0), (0, 4, 2), (4, 1, 0, 0), (0, 3, 1), (0, 0, 6), (4, 2, 3, 1), (4, 0, 0, 6), (0, 2, 2),
        (2, 0, 0, 1, 0), (4, 1, 0, 6), (2, 0, 6, 2, 2), (0, 1, 2), (4, 2, 1, 2), (0, 4, 3), (4, 1, 1, 2), (0, 4, 4),
        (0, 4, 7), (4, 0, 0, 0), (0, 1, 1), (0, 0, 1), (2, 1, 2, 3, 1), (0, 4, 5), (0, 0, 4), (4, 1, 0, 4),
        (4, 2, 0, 4), (4, 0, 3, 1), (0, 3, 2), (0, 2, 6), (0, 3, 6), (4, 0, 2, 6), (0, 0, 7), (0, 1, 6),
        (2, 1, 1, 0, 1), (2, 0, 7, 1, 6), (0, 2, 7), (4, 0, 1, 6), (0, 1, 3), (1, 1, 1), (4, 2, 3, 2), (0, 3, 3),
        (4, 2, 3, 3), (1, 0, 7), (2, 1, 3, 2, 6), (0, 0, 5), (0, 2, 4), (4, 2, 2, 4), (2, 3, 3, 3, 6), (2, 0, 5, 2, 4),
        (0, 1, 4), (4, 1, 1, 4), (4, 2, 1, 4), (0, 3, 7), (4, 0, 3, 7), (1, 0, 1), (4, 2, 2, 2), (0, 0, 2),
        (4, 0, 3, 6), (2, 2, 7, 0, 4), (2, 3, 7, 0, 2), (4, 1, 0, 2), (4, 2, 0, 2), (0, 1, 5), (0, 3, 5), (1, 0, 5),
        (4, 0, 2, 7), (2, 3, 2, 1, 4), (2, 3, 5, 1, 5), (0, 3, 4), (4, 2, 3, 4), (1, 1, 3), (1, 3, 2), (0, 0, 3),
        (4, 2, 2, 0), (0, 2, 5), (1, 3, 3), (2, 0, 3, 3, 4), (1, 1, 5), (4, 2, 2, 5), (1, 2, 4), (4, 1, 1, 6),
        (4, 2, 3, 5), (1, 1, 2), (1, 3, 1), (1, 0, 4), (1, 2, 6), (4, 1, 2, 2), (0, 1, 7), (1, 3, 4),
        (2, 1, 7, 2, 5), (1, 1, 0), (1, 3, 0), (4, 1, 2, 0), (1, 0, 6), (1, 1, 7), (0, 2, 3), (1, 2, 5),
        (1, 3, 6), (1, 0, 3), (0, 2, 1), (1, 3, 5), (2, 2, 3, 2, 1), (1, 2, 7), (1, 1, 4), (1, 2, 3),
        (1, 2, 1), (1, 3, 7), (1, 0, 2), (1, 1, 6), (1, 2, 2), (1, 0, 0), (1, 2, 0),
    ),
)

PARTS = len(SPLIT)
STARTS = tuple(sum(SPLIT[:part]) for part in range(PARTS))


def place_of(dz, dy):
    return dz % DEPTH * 2 + dy


def spot_of(kind, place):
    dz, dy = place // 2, place % 2
    return (dz - DEPTH if kind == 1 and dz == DEPTH - 1 else dz), dy


def along_z(kind):
    return {1: INWARD} if kind == 0 else {1: INWARD, -1: OUTWARD}


def across_last(kind, part, place):
    dz, _ = spot_of(kind, place)
    near = dz in (0, DEPTH - 1) if kind == 0 else dz in (0, 1)
    return ACROSS_LAST[kind if near else 1 - kind][part]


def onward(kind, part, place):
    dz, dy = spot_of(kind, place)
    links = along_z(kind)
    ways = (1, -1) if dz == 0 else ((-1,) if dz > 0 else (1,))
    depth_links = [links[way] for way in ways if way in links]
    if across_last(kind, part, place):
        return depth_links + [ACROSS] if dy == 0 else []
    return ([ACROSS] if dz == 0 and dy == 0 else []) + depth_links


def back(kind, part, place):
    dz, dy = spot_of(kind, place)
    if dy == 1 and (across_last(kind, part, place) or dz == 0):
        return ACROSS
    return along_z(kind)[1 if dz > 0 else -1]


def beyond(kind, link, place):
    dz, dy = spot_of(kind, place)
    if link == ACROSS:
        return kind, place_of(dz, 1 - dy), ACROSS
    if kind == 0:
        return 1, place_of(dz - 1, dy), OUTWARD
    if link == INWARD:
        return 1, place_of(1 - dz, dy), INWARD
    return 0, place_of(dz + 1, dy), INWARD


def grid_kernel(
    x_hbm, gain_hbm, router_hbm, ids_hbm, gate_hbm, up_hbm, down_hbm, out_ref,
    x_ref, gain_ref, router_ref, ids_ref, gate_w, up_w, down_w, xg, yb, ys, arrived, hb, routes, route_col,
    in_sem, load_sem, ag_s, ag_r, sx_s, sx_r, sy_s, sy_r, rs_s, rs_r, rt_s, rt_r, rx_s, rx_r,
):
    rows, width = x_ref.shape
    me = lax.axis_index("expert")
    core = me % 2
    y_at = (me // 2) % 2
    z_at = me // 4
    is_corner = z_at % 3 == 0
    sibling = me + 1 - 2 * core

    def device_at(z, y):
        return (z * 2 + y) * 2 + core

    across = device_at(z_at, 1 - y_at)
    neighbours = (
        (device_at(1 + z_at // 3, y_at), across),
        (device_at(3 - z_at, y_at), across, device_at(3 * (z_at - 1), y_at)),
    )

    def by_kind(body):
        for kind in range(2):
            pl.when(is_corner if kind == 0 else jnp.logical_not(is_corner))(lambda kind=kind: body(kind))

    def greet(kind):
        for device in neighbours[kind] + (sibling,):
            pl.semaphore_signal(
                barrier, inc=1, device_id={"expert": device}, device_id_type=pl.DeviceIdType.MESH
            )

    def remote(src, dst, send, recv, device):
        return pltpu.make_async_remote_copy(
            src_ref=src, dst_ref=dst, send_sem=send, recv_sem=recv,
            device_id={"expert": device}, device_id_type=pl.DeviceIdType.MESH,
        )

    def grains(part, place):
        return pl.ds(place * (rows // GRAIN) + STARTS[part], SPLIT[part])

    def number(part, place):
        return place * PARTS + part

    def gather_copy(kind, link, part, place):
        _, there, _ = beyond(kind, link, place)
        return remote(
            xg.at[0, grains(part, place)], xg.at[0, grains(part, there)],
            ag_s.at[link], ag_r.at[number(part, there)], neighbours[kind][link],
        )

    def gathered(part, place):
        at, slot = number(part, place), grains(part, place)
        return remote(xg.at[0, slot], xg.at[0, slot], ag_s.at[0], ag_r.at[at], sibling)

    def sibling_x(part, place):
        at, slot = number(part, place), grains(part, place)
        return remote(xg.at[0, slot], xg.at[1, slot], sx_s.at[0], sx_r.at[at], sibling)

    def sibling_y(part, place):
        at, slot = number(part, place), grains(part, place)
        return remote(yb.at[1, slot], ys.at[slot], sy_s.at[0], sy_r.at[at], sibling)

    def route_copy(kind, link, place):
        _, there, _ = beyond(kind, link, place)
        return remote(
            routes.at[0, place], routes.at[0, there], rt_s.at[link], rt_r.at[there],
            neighbours[kind][link],
        )

    def routed(place):
        return remote(routes.at[0, place], routes.at[0, place], rt_s.at[0], rt_r.at[place], sibling)

    def sibling_route(place):
        return remote(routes.at[0, place], routes.at[1, place], rx_s.at[0], rx_r.at[place], sibling)

    def reduce_copy(kind, part, place):
        link = back(kind, part, place)
        _, there, entry = beyond(kind, link, place)
        return remote(
            yb.at[0, grains(part, place)], arrived.at[entry, grains(part, there)],
            rs_s.at[0], rs_r.at[entry, number(part, there)], neighbours[kind][link],
        )

    def reduced(link, part, place):
        at, slot = number(part, place), grains(part, place)
        return remote(yb.at[0, slot], arrived.at[link, slot], rs_s.at[0], rs_r.at[link, at], sibling)

    def in_copy(part):
        part_rows = pl.ds(STARTS[part] * GRAIN, SPLIT[part] * GRAIN)
        return pltpu.make_async_copy(x_hbm.at[part_rows], x_ref.at[part_rows], in_sem.at[part])

    def norm(part):
        in_copy(part).wait()
        first, last = STARTS[part], STARTS[part] + SPLIT[part]
        as_float = x_ref[first * GRAIN : last * GRAIN].astype(jnp.float32)
        inv_rms = lax.rsqrt(jnp.mean(as_float * as_float, axis=1, keepdims=True) + 1e-06)
        normed = (as_float * inv_rms * gain_ref[...]).astype(jnp.bfloat16)
        xg[0, first:last] = normed.reshape(last - first, GRAIN, width)

    def arrive(kind, part, place):
        if part == PARTS:
            if place != 0:
                routed(place).wait_recv()
            for link in onward(kind, part, place):
                route_copy(kind, link, place).start()
            sibling_route(place).start()
            return
        if place != 0:
            gathered(part, place).wait_recv()
        sibling_x(part, place).start()

    def send(kind, link, part, place):
        gather_copy(kind, link, part, place).start()

    def reduce(kind, part, place):
        sibling_y(part, place).wait_recv()
        links = onward(kind, part, place)
        for link in links:
            reduced(link, part, place).wait_recv()
        for grain in range(SPLIT[part]):
            at = place * (rows // GRAIN) + STARTS[part] + grain
            value = yb[0, at].astype(jnp.float32) + ys[at].astype(jnp.float32)
            for link in links:
                value = value + arrived[link, at].astype(jnp.float32)
            value = value.astype(jnp.bfloat16)
            if place == 0:
                first = (STARTS[part] + grain) * GRAIN
                out_ref[first : first + GRAIN] = value
            else:
                yb[0, at] = value
        if place != 0:
            reduce_copy(kind, part, place).start()

    diagonal = lax.broadcasted_iota(jnp.int32, (rows, rows), 0) == lax.broadcasted_iota(
        jnp.int32, (rows, rows), 1
    )

    def columns_of(place):
        sibling_route(place).wait_recv()
        for lane in range(2):
            values = routes[lane, place, pl.ds(me, 1), :]
            column = jnp.sum(jnp.where(diagonal, values, 0.0), axis=1, keepdims=True)
            spread = jnp.broadcast_to(column, (rows, rows))
            for grain in range(rows // GRAIN):
                at = place * (rows // GRAIN) + grain
                route_col[lane, at] = spread[grain * GRAIN : (grain + 1) * GRAIN]

    def route():
        logits = lax.dot_general(
            router_ref[...], xg[0, : rows // GRAIN].reshape(rows, width), (((1,), (1,)), ((), ())),
            preferred_element_type=jnp.float32,
        )
        exp_logits = jnp.exp(logits)
        expert_iota = lax.broadcasted_iota(jnp.int32, logits.shape, 0)
        chosen = expert_iota < 0
        for k in range(ids_ref.shape[0]):
            chosen = chosen | (ids_ref[k : k + 1, :] == expert_iota)
        picked = jnp.where(chosen, exp_logits, 0.0)
        routes[0, 0] = picked / jnp.sum(picked, axis=0, keepdims=True)

    def compute(corner_grains, middle_grains):
        at = [jnp.where(is_corner, a, b) for a, b in zip(corner_grains, middle_grains)]
        x = jnp.concatenate([xg[lane, a] for lane in range(2) for a in at], axis=0)
        gate = jnp.dot(x, gate_w[...], preferred_element_type=jnp.float32)
        up = jnp.dot(x, up_w[...], preferred_element_type=jnp.float32)
        hb[...] = (gate / (1.0 + jnp.exp(-gate)) * up).astype(jnp.bfloat16)
        y = jnp.dot(hb[...], down_w[...], preferred_element_type=jnp.float32)
        for lane in range(2):
            for i, a in enumerate(at):
                first = (lane * GROUP + i) * GRAIN
                weight = jnp.concatenate([route_col[lane, a]] * (width // rows), axis=1)
                yb[lane, a] = (y[first : first + GRAIN] * weight).astype(jnp.bfloat16)

    barrier = pltpu.get_barrier_semaphore()

    cuts = [[[]], [[]]]
    shared = [[], []]
    seen = [set(), set()]
    for kind in range(2):
        normed, greeted = set(), False
        for step in STEPS[kind]:
            own = step[1:2] if step[0] == ARRIVE and step[2] == 0 else ()
            for part in range(PARTS) if step[0] == ROUTE else own:
                if part < PARTS and part not in normed:
                    normed.add(part)
                    cuts[kind][-1].append((norm, part))
            if not greeted:
                greeted = True
                cuts[kind][-1].append((pl.semaphore_wait, barrier, len(neighbours[kind]) + 1))
            if step[0] == ROUTE:
                shared[kind].append(None)
                cuts[kind].append([])
            elif step[0] == COMPUTE:
                pieces = [(step[i], step[i + 1]) for i in range(1, len(step), 2)]
                for part, place in pieces:
                    cuts[kind][-1].append((sibling_x(part, place).wait_recv,))
                    if place not in seen[kind]:
                        seen[kind].add(place)
                        cuts[kind][-1].append((columns_of, place))
                shared[kind].append(
                    [place * (rows // GRAIN) + STARTS[part] + i for part, place in pieces for i in range(SPLIT[part])]
                )
                cuts[kind].append([(sibling_y(part, place).start,) for part, place in pieces])
            else:
                cuts[kind][-1].append(({ARRIVE: arrive, REDUCE: reduce, SEND: send}[step[0]], kind, *step[1:]))

    def section(index):
        def body(kind):
            for action, *details in cuts[kind][index]:
                action(*details)

        by_kind(body)

    def finish(kind):
        for link, device in enumerate(neighbours[kind]):
            sent = sum(
                SPLIT[part]
                for place in range(2 * DEPTH)
                for part in range(PARTS)
                if link in onward(kind, part, place)
            )
            slot = xg.at[0, pl.ds(0, sent)]
            remote(slot, slot, ag_s.at[link], ag_r.at[0], device).wait_send()
            sent = sum(link in onward(kind, PARTS, place) for place in range(2 * DEPTH))
            if sent:
                slot = routes.at[0, pl.ds(0, sent)]
                remote(slot, slot, rt_s.at[link], rt_r.at[0], device).wait_send()
        remote(xg.at[0], xg.at[1], sx_s.at[0], sx_r.at[0], sibling).wait_send()
        remote(yb.at[1], ys, sy_s.at[0], sy_r.at[0], sibling).wait_send()
        remote(routes.at[0], routes.at[1], rx_s.at[0], rx_r.at[0], sibling).wait_send()
        returned = pl.ds(rows // GRAIN, (2 * DEPTH - 1) * (rows // GRAIN))
        remote(yb.at[0, returned], ys.at[returned], rs_s.at[0], rs_r.at[0, 0], sibling).wait_send()

    by_kind(greet)
    small = [
        pltpu.make_async_copy(src, dst, in_sem.at[PARTS + i])
        for i, (src, dst) in enumerate(((gain_hbm, gain_ref), (router_hbm, router_ref), (ids_hbm, ids_ref)))
    ]
    small[0].start()
    for part in range(PARTS):
        in_copy(part).start()
    for copy in small[1:]:
        copy.start()
    loads = [
        pltpu.make_async_copy(src.at[0], dst, load_sem.at[i])
        for i, (src, dst) in enumerate(((gate_hbm, gate_w), (up_hbm, up_w), (down_hbm, down_w)))
    ]
    for load in loads:
        load.start()
    small[0].wait()
    first = True
    for index, (corner, middle) in enumerate(zip(*shared)):
        section(index)
        if corner is None:
            for copy in small[1:]:
                copy.wait()
            route()
        else:
            if first:
                first = False
                for load in loads:
                    load.wait()
            compute(corner, middle)
    section(len(shared[0]))
    by_kind(finish)


def grid_local(hidden_in, norm_gain, router_weight, expert_ids, w_gate, w_up, w_down):
    rows, width = hidden_in.shape
    ff = w_gate.shape[2]
    count = router_weight.shape[1]
    places = 2 * DEPTH
    total = places * rows // GRAIN
    hbm = pl.BlockSpec(memory_space=pl.ANY)
    dma = pltpu.SemaphoreType.DMA
    pieces = places * PARTS
    return pl.pallas_call(
        grid_kernel,
        out_shape=pltpu.VMEM((rows, width), jnp.bfloat16),
        in_specs=[hbm] * 7,
        out_specs=pl.BlockSpec(memory_space=pltpu.VMEM),
        scratch_shapes=[
            pltpu.VMEM((rows, width), jnp.bfloat16),
            pltpu.VMEM((1, width), jnp.float32),
            pltpu.VMEM((count, width), jnp.bfloat16),
            pltpu.VMEM(expert_ids.shape[::-1], jnp.int32),
            pltpu.VMEM((width, ff), jnp.bfloat16),
            pltpu.VMEM((width, ff), jnp.bfloat16),
            pltpu.VMEM((ff, width), jnp.bfloat16),
            pltpu.VMEM((2, total, GRAIN, width), jnp.bfloat16),
            pltpu.VMEM((2, total, GRAIN, width), jnp.bfloat16),
            pltpu.VMEM((total, GRAIN, width), jnp.bfloat16),
            pltpu.VMEM((3, total, GRAIN, width), jnp.bfloat16),
            pltpu.VMEM((2 * GROUP * GRAIN, ff), jnp.bfloat16),
            pltpu.VMEM((2, places, count, rows), jnp.float32),
            pltpu.VMEM((2, total, GRAIN, rows), jnp.float32),
            dma((PARTS + 3,)), dma((3,)), dma((3,)), dma((pieces,)), dma((1,)), dma((pieces,)),
            dma((1,)), dma((pieces,)), dma((1,)), dma((3, pieces)),
            dma((3,)), dma((places,)), dma((1,)), dma((places,)),
        ],
        compiler_params=pltpu.CompilerParams(
            collective_id=0, has_side_effects=True, vmem_limit_bytes=56 * 1024 * 1024
        ),
    )(hidden_in, norm_gain.reshape(1, width), router_weight.T, expert_ids.T, w_gate, w_up, w_down)


def local(hidden_in, norm_gain, router_weight, expert_ids, w_gate, w_up, w_down):
    tok_rows, width = hidden_in.shape
    top_count = expert_ids.shape[1]
    num_experts = router_weight.shape[1]
    dev_count = lax.axis_size("expert")
    local_experts = w_gate.shape[0]
    cap_rows = tok_rows * top_count * 3 // (2 * num_experts)
    as_float = hidden_in.astype(jnp.float32)
    inv_rms = lax.rsqrt(jnp.mean(as_float * as_float, axis=1, keepdims=True) + 1e-06)
    normed = (as_float * inv_rms * norm_gain).astype(jnp.bfloat16)
    logits = jnp.dot(normed, router_weight, preferred_element_type=jnp.float32)
    expert_iota = jnp.arange(num_experts, dtype=jnp.int32)
    chosen = jnp.any(expert_ids[:, :, None] == expert_iota[None, None, :], axis=1)
    picked = jnp.where(chosen, jnp.exp(logits), 0.0)
    route_w = picked / jnp.sum(picked, axis=1, keepdims=True)
    earlier = jnp.arange(tok_rows)[:, None] > jnp.arange(tok_rows)[None, :]
    slot_index = jnp.dot(
        earlier.astype(jnp.float32), chosen.astype(jnp.float32), precision=lax.Precision.HIGHEST
    ).astype(jnp.int32)
    dispatch = chosen[:, :, None] & (slot_index[:, :, None] == jnp.arange(cap_rows)[None, None, :])
    outgoing = jnp.einsum(
        "tes,td->esd", dispatch.astype(jnp.bfloat16), normed, preferred_element_type=jnp.float32
    ).astype(jnp.bfloat16)
    arrived = lax.all_to_all(
        outgoing.reshape(dev_count, local_experts, cap_rows, width), "expert", 0, 0, tiled=True
    )
    gate_act = jnp.einsum("semd,edf->semf", arrived, w_gate, preferred_element_type=jnp.float32)
    up_act = jnp.einsum("semd,edf->semf", arrived, w_up, preferred_element_type=jnp.float32)
    hidden = (jax.nn.silu(gate_act) * up_act).astype(jnp.bfloat16)
    expert_out = jnp.einsum("semf,efd->semd", hidden, w_down, preferred_element_type=jnp.float32)
    returned = lax.all_to_all(expert_out.astype(jnp.bfloat16), "expert", 0, 0, tiled=True)
    combined = jnp.einsum(
        "tes,esd->td",
        jnp.where(dispatch, route_w[:, :, None], 0.0),
        returned.reshape(num_experts, cap_rows, width).astype(jnp.float32),
        precision=lax.Precision.HIGHEST,
    )
    return combined.astype(jnp.bfloat16)


def solution(mesh):
    in_specs = (
        P(("groups", "expert"), None),
        P(),
        P(),
        P(("groups", "expert"), None),
        P("expert", None, None),
        P("expert", None, None),
        P("expert", None, None),
    )
    out_specs = P(("groups", "expert"), None)
    gridded = mesh.shape["expert"] == 4 * DEPTH
    body = grid_local if gridded else local
    return jax.shard_map(body, mesh=mesh, in_specs=in_specs, out_specs=out_specs, check_vma=False)
```

```python
import jax
import jax.numpy as jnp
from jax import lax
from jax.experimental import pallas as pl
from jax.experimental.pallas import tpu as pltpu
from jax.sharding import PartitionSpec as P

DEPTH = 4
GRAIN = 16
GROUP = 4
INWARD, ACROSS, OUTWARD = range(3)
ARRIVE, REDUCE, COMPUTE, ROUTE, SEND = range(5)

SPLIT = (2, 2, 1, 2, 1)
ACROSS_LAST = (
    (True, True, True, False, False, False),
    (True, True, True, False, False, False),
)
STEPS = (
    (
        (0, 2, 0), (3,), (0, 5, 0), (0, 1, 0), (4, 0, 1, 0), (0, 0, 0), (4, 1, 0, 0), (4, 1, 1, 0),
        (0, 4, 0), (4, 0, 4, 0), (4, 0, 2, 0), (0, 3, 0), (4, 0, 3, 0), (4, 1, 4, 0), (0, 5, 1), (0, 5, 2),
        (2, 3, 0, 0, 0), (4, 1, 3, 0), (4, 0, 0, 0), (2, 2, 0, 1, 0, 4, 0), (0, 1, 2), (4, 1, 1, 2), (0, 0, 1), (0, 1, 1),
        (2, 0, 1, 1, 2), (0, 5, 4), (0, 5, 3), (0, 3, 2), (0, 4, 1), (0, 4, 2), (4, 0, 4, 1), (4, 1, 2, 0),
        (1, 0, 1), (2, 1, 1, 3, 2), (0, 4, 3), (0, 3, 1), (4, 0, 3, 1), (1, 1, 1), (1, 3, 2), (2, 3, 1, 4, 1, 4, 3),
        (0, 5, 5), (0, 5, 6), (0, 1, 3), (0, 0, 4), (4, 1, 0, 4), (0, 2, 1), (1, 4, 3), (2, 0, 4, 1, 3),
        (0, 3, 3), (1, 1, 3), (2, 2, 1, 3, 3, 4, 2), (0, 1, 6), (0, 4, 4), (4, 1, 1, 6), (1, 4, 2), (1, 3, 3),
        (0, 2, 6), (2, 2, 6, 4, 4, 1, 6), (0, 0, 5), (4, 1, 2, 6), (1, 2, 1), (0, 3, 5), (1, 4, 4), (1, 1, 2),
        (0, 4, 7), (2, 3, 5, 0, 5), (0, 5, 7), (0, 4, 5), (0, 1, 7), (1, 0, 5), (1, 3, 5), (2, 1, 7, 4, 7, 4, 5),
        (0, 2, 7), (0, 0, 6), (4, 1, 0, 6), (1, 4, 7), (1, 4, 5), (1, 1, 7), (0, 3, 6), (1, 0, 4),
        (0, 4, 6), (2, 4, 6, 3, 6, 2, 7), (0, 0, 7), (0, 1, 4), (4, 1, 1, 4), (1, 4, 6), (2, 0, 7, 0, 6), (1, 3, 6),
        (1, 1, 6), (0, 3, 7), (1, 2, 7), (1, 0, 7), (2, 1, 4, 3, 7), (0, 1, 5), (0, 2, 4), (4, 1, 2, 4),
        (1, 3, 7), (1, 2, 6), (0, 0, 2), (4, 1, 0, 2), (2, 1, 5, 0, 2), (0, 2, 2), (4, 1, 2, 2), (1, 0, 6),
        (1, 1, 5), (0, 2, 5), (0, 3, 4), (2, 3, 4, 2, 5, 2, 2), (0, 0, 3), (1, 4, 1), (1, 2, 5), (1, 3, 4),
        (0, 2, 3), (2, 2, 3, 0, 3, 2, 4), (1, 1, 4), (1, 2, 3), (1, 0, 3), (1, 4, 0), (1, 2, 4), (1, 1, 0),
        (1, 2, 2), (1, 3, 1), (1, 0, 2), (1, 2, 0), (1, 3, 0), (1, 0, 0),
    ),
    (
        (0, 2, 0), (3,), (0, 4, 0), (0, 5, 0), (0, 0, 0), (0, 3, 0), (4, 0, 0, 0), (0, 1, 0),
        (4, 2, 1, 0), (4, 1, 4, 0), (4, 0, 4, 0), (4, 1, 3, 0), (4, 1, 1, 0), (4, 2, 3, 0), (4, 0, 1, 0), (0, 5, 6),
        (0, 5, 2), (0, 5, 1), (4, 2, 4, 0), (2, 1, 0, 4, 0, 2, 0), (0, 1, 6), (4, 0, 1, 6), (0, 0, 2), (4, 1, 0, 2),
        (0, 4, 1), (4, 2, 4, 1), (2, 3, 0, 0, 0), (4, 2, 0, 2), (4, 1, 1, 6), (4, 0, 4, 1), (0, 4, 6), (0, 3, 1),
        (0, 2, 6), (2, 0, 2, 1, 6), (0, 1, 1), (0, 5, 4), (4, 0, 4, 6), (0, 5, 3), (4, 1, 2, 6), (4, 0, 2, 6),
        (4, 2, 3, 1), (0, 5, 7), (0, 1, 2), (4, 1, 1, 2), (2, 2, 6, 3, 1, 4, 1), (0, 0, 3), (4, 0, 3, 1), (0, 1, 4),
        (4, 1, 1, 4), (0, 0, 6), (4, 2, 1, 4), (0, 3, 6), (0, 4, 2), (0, 4, 3), (2, 0, 3, 1, 1), (0, 1, 7),
        (0, 4, 7), (4, 0, 4, 7), (0, 4, 4), (0, 2, 7), (4, 1, 0, 6), (4, 2, 4, 2), (0, 2, 4), (4, 2, 2, 4),
        (2, 4, 7, 4, 3, 0, 6), (2, 4, 4, 2, 4, 2, 7, 4, 2), (0, 3, 3), (4, 1, 2, 4), (4, 2, 3, 3), (1, 0, 3), (0, 4, 5), (4, 2, 4, 5),
        (0, 1, 3), (0, 5, 5), (0, 1, 5), (4, 2, 4, 3), (4, 0, 0, 6), (4, 0, 3, 6), (0, 3, 7), (2, 1, 4, 3, 3),
        (4, 0, 3, 7), (2, 3, 7, 4, 5, 4, 6), (0, 2, 5), (0, 0, 4), (4, 1, 0, 4), (0, 0, 7), (4, 2, 0, 4), (2, 1, 3, 1, 5),
        (1, 2, 7), (0, 3, 4), (4, 2, 3, 4), (4, 2, 4, 4), (4, 1, 2, 0), (4, 1, 0, 0), (4, 0, 2, 0), (4, 0, 3, 0),
        (1, 4, 2), (4, 2, 1, 2), (1, 1, 5), (0, 3, 5), (0, 0, 5), (2, 0, 5, 3, 5), (0, 2, 2), (4, 2, 3, 5),
        (4, 1, 2, 2), (0, 2, 1), (1, 3, 3), (2, 2, 2, 2, 5, 3, 4), (1, 4, 5), (1, 0, 5), (0, 0, 1), (4, 2, 2, 2),
        (4, 2, 0, 0), (2, 0, 7, 1, 7), (1, 2, 5), (1, 4, 3), (1, 1, 3), (4, 2, 2, 0), (0, 3, 2), (1, 0, 2),
        (4, 2, 3, 2), (0, 2, 3), (1, 4, 4), (2, 3, 6, 2, 1, 2, 3), (1, 0, 7), (2, 0, 4, 1, 2), (1, 2, 3), (1, 3, 4),
        (2, 0, 1, 3, 2), (1, 1, 7), (1, 4, 6), (1, 1, 4), (1, 4, 7), (1, 0, 1), (1, 3, 6), (1, 3, 5),
        (1, 2, 4), (1, 4, 1), (1, 2, 1), (1, 0, 4), (1, 3, 1), (1, 1, 6), (1, 3, 7), (1, 2, 6),
        (1, 3, 2), (1, 1, 1), (1, 4, 0), (1, 0, 6), (1, 1, 2), (1, 2, 2), (1, 3, 0), (1, 1, 0),
        (1, 2, 0), (1, 0, 0),
    ),
)

PARTS = len(SPLIT)
STARTS = tuple(sum(SPLIT[:part]) for part in range(PARTS))


def place_of(dz, dy):
    return dz % DEPTH * 2 + dy


def spot_of(kind, place):
    dz, dy = place // 2, place % 2
    return (dz - DEPTH if kind == 1 and dz == DEPTH - 1 else dz), dy


def along_z(kind):
    return {1: INWARD} if kind == 0 else {1: INWARD, -1: OUTWARD}


def across_last(kind, part, place):
    dz, _ = spot_of(kind, place)
    near = dz in (0, DEPTH - 1) if kind == 0 else dz in (0, 1)
    return ACROSS_LAST[kind if near else 1 - kind][part]


def onward(kind, part, place):
    dz, dy = spot_of(kind, place)
    links = along_z(kind)
    ways = (1, -1) if dz == 0 else ((-1,) if dz > 0 else (1,))
    depth_links = [links[way] for way in ways if way in links]
    if across_last(kind, part, place):
        return depth_links + [ACROSS] if dy == 0 else []
    return ([ACROSS] if dz == 0 and dy == 0 else []) + depth_links


def back(kind, part, place):
    dz, dy = spot_of(kind, place)
    if dy == 1 and (across_last(kind, part, place) or dz == 0):
        return ACROSS
    return along_z(kind)[1 if dz > 0 else -1]


def beyond(kind, link, place):
    dz, dy = spot_of(kind, place)
    if link == ACROSS:
        return kind, place_of(dz, 1 - dy), ACROSS
    if kind == 0:
        return 1, place_of(dz - 1, dy), OUTWARD
    if link == INWARD:
        return 1, place_of(1 - dz, dy), INWARD
    return 0, place_of(dz + 1, dy), INWARD


def grid_kernel(
    x_hbm, gain_hbm, router_hbm, ids_hbm, gate_hbm, up_hbm, down_hbm, out_ref,
    x_ref, gain_ref, router_ref, ids_ref, gate_w, up_w, down_w, xg, yb, ys, arrived, hb, routes, route_col,
    in_sem, load_sem, ag_s, ag_r, sx_s, sx_r, sy_s, sy_r, rs_s, rs_r, rt_s, rt_r, rx_s, rx_r,
):
    rows, width = x_ref.shape
    me = lax.axis_index("expert")
    core = me % 2
    y_at = (me // 2) % 2
    z_at = me // 4
    is_corner = z_at % 3 == 0
    sibling = me + 1 - 2 * core

    def device_at(z, y):
        return (z * 2 + y) * 2 + core

    across = device_at(z_at, 1 - y_at)
    neighbours = (
        (device_at(1 + z_at // 3, y_at), across),
        (device_at(3 - z_at, y_at), across, device_at(3 * (z_at - 1), y_at)),
    )

    def by_kind(body):
        for kind in range(2):
            pl.when(is_corner if kind == 0 else jnp.logical_not(is_corner))(lambda kind=kind: body(kind))

    def greet(kind):
        for device in neighbours[kind] + (sibling,):
            pl.semaphore_signal(
                barrier, inc=1, device_id={"expert": device}, device_id_type=pl.DeviceIdType.MESH
            )

    def remote(src, dst, send, recv, device):
        return pltpu.make_async_remote_copy(
            src_ref=src, dst_ref=dst, send_sem=send, recv_sem=recv,
            device_id={"expert": device}, device_id_type=pl.DeviceIdType.MESH,
        )

    def grains(part, place):
        return pl.ds(place * (rows // GRAIN) + STARTS[part], SPLIT[part])

    def number(part, place):
        return place * PARTS + part

    def gather_copy(kind, link, part, place):
        _, there, _ = beyond(kind, link, place)
        return remote(
            xg.at[0, grains(part, place)], xg.at[0, grains(part, there)],
            ag_s.at[link], ag_r.at[number(part, there)], neighbours[kind][link],
        )

    def gathered(part, place):
        at, slot = number(part, place), grains(part, place)
        return remote(xg.at[0, slot], xg.at[0, slot], ag_s.at[0], ag_r.at[at], sibling)

    def sibling_x(part, place):
        at, slot = number(part, place), grains(part, place)
        return remote(xg.at[0, slot], xg.at[1, slot], sx_s.at[0], sx_r.at[at], sibling)

    def sibling_y(part, place):
        at, slot = number(part, place), grains(part, place)
        return remote(yb.at[1, slot], ys.at[slot], sy_s.at[0], sy_r.at[at], sibling)

    def route_copy(kind, link, place):
        _, there, _ = beyond(kind, link, place)
        return remote(
            routes.at[0, place], routes.at[0, there], rt_s.at[link], rt_r.at[there],
            neighbours[kind][link],
        )

    def routed(place):
        return remote(routes.at[0, place], routes.at[0, place], rt_s.at[0], rt_r.at[place], sibling)

    def sibling_route(place):
        return remote(routes.at[0, place], routes.at[1, place], rx_s.at[0], rx_r.at[place], sibling)

    def reduce_copy(kind, part, place):
        link = back(kind, part, place)
        _, there, entry = beyond(kind, link, place)
        return remote(
            yb.at[0, grains(part, place)], arrived.at[entry, grains(part, there)],
            rs_s.at[0], rs_r.at[entry, number(part, there)], neighbours[kind][link],
        )

    def reduced(link, part, place):
        at, slot = number(part, place), grains(part, place)
        return remote(yb.at[0, slot], arrived.at[link, slot], rs_s.at[0], rs_r.at[link, at], sibling)

    def in_copy(part):
        part_rows = pl.ds(STARTS[part] * GRAIN, SPLIT[part] * GRAIN)
        return pltpu.make_async_copy(x_hbm.at[part_rows], x_ref.at[part_rows], in_sem.at[part])

    def norm(part):
        in_copy(part).wait()
        first, last = STARTS[part], STARTS[part] + SPLIT[part]
        as_float = x_ref[first * GRAIN : last * GRAIN].astype(jnp.float32)
        inv_rms = lax.rsqrt(jnp.mean(as_float * as_float, axis=1, keepdims=True) + 1e-06)
        normed = (as_float * inv_rms * gain_ref[...]).astype(jnp.bfloat16)
        xg[0, first:last] = normed.reshape(last - first, GRAIN, width)

    def arrive(kind, part, place):
        if part == PARTS:
            if place != 0:
                routed(place).wait_recv()
            for link in onward(kind, part, place):
                route_copy(kind, link, place).start()
            sibling_route(place).start()
            return
        if place != 0:
            gathered(part, place).wait_recv()
        sibling_x(part, place).start()

    def send(kind, link, part, place):
        gather_copy(kind, link, part, place).start()

    def reduce(kind, part, place):
        sibling_y(part, place).wait_recv()
        links = onward(kind, part, place)
        for link in links:
            reduced(link, part, place).wait_recv()
        for grain in range(SPLIT[part]):
            at = place * (rows // GRAIN) + STARTS[part] + grain
            value = yb[0, at].astype(jnp.float32) + ys[at].astype(jnp.float32)
            for link in links:
                value = value + arrived[link, at].astype(jnp.float32)
            value = value.astype(jnp.bfloat16)
            if place == 0:
                first = (STARTS[part] + grain) * GRAIN
                out_ref[first : first + GRAIN] = value
            else:
                yb[0, at] = value
        if place != 0:
            reduce_copy(kind, part, place).start()

    diagonal = lax.broadcasted_iota(jnp.int32, (rows, rows), 0) == lax.broadcasted_iota(
        jnp.int32, (rows, rows), 1
    )

    def columns_of(place):
        sibling_route(place).wait_recv()
        for lane in range(2):
            values = routes[lane, place, pl.ds(me, 1), :]
            column = jnp.sum(jnp.where(diagonal, values, 0.0), axis=1, keepdims=True)
            spread = jnp.broadcast_to(column, (rows, rows))
            for grain in range(rows // GRAIN):
                at = place * (rows // GRAIN) + grain
                route_col[lane, at] = spread[grain * GRAIN : (grain + 1) * GRAIN]

    def route():
        logits = lax.dot_general(
            router_ref[...], xg[0, : rows // GRAIN].reshape(rows, width), (((1,), (1,)), ((), ())),
            preferred_element_type=jnp.float32,
        )
        exp_logits = jnp.exp(logits)
        expert_iota = lax.broadcasted_iota(jnp.int32, logits.shape, 0)
        chosen = expert_iota < 0
        for k in range(ids_ref.shape[0]):
            chosen = chosen | (ids_ref[k : k + 1, :] == expert_iota)
        picked = jnp.where(chosen, exp_logits, 0.0)
        routes[0, 0] = picked / jnp.sum(picked, axis=0, keepdims=True)

    def compute(corner_grains, middle_grains):
        at = [jnp.where(is_corner, a, b) for a, b in zip(corner_grains, middle_grains)]
        x = jnp.concatenate([xg[lane, a] for lane in range(2) for a in at], axis=0)
        gate = jnp.dot(x, gate_w[...], preferred_element_type=jnp.float32)
        up = jnp.dot(x, up_w[...], preferred_element_type=jnp.float32)
        hb[...] = (gate / (1.0 + jnp.exp(-gate)) * up).astype(jnp.bfloat16)
        y = jnp.dot(hb[...], down_w[...], preferred_element_type=jnp.float32)
        for lane in range(2):
            for i, a in enumerate(at):
                first = (lane * GROUP + i) * GRAIN
                weight = jnp.concatenate([route_col[lane, a]] * (width // rows), axis=1)
                yb[lane, a] = (y[first : first + GRAIN] * weight).astype(jnp.bfloat16)

    barrier = pltpu.get_barrier_semaphore()

    cuts = [[[]], [[]]]
    shared = [[], []]
    seen = [set(), set()]
    for kind in range(2):
        normed, greeted = set(), False
        for step in STEPS[kind]:
            own = step[1:2] if step[0] == ARRIVE and step[2] == 0 else ()
            for part in range(PARTS) if step[0] == ROUTE else own:
                if part < PARTS and part not in normed:
                    normed.add(part)
                    cuts[kind][-1].append((norm, part))
            if not greeted:
                greeted = True
                cuts[kind][-1].append((pl.semaphore_wait, barrier, len(neighbours[kind]) + 1))
            if step[0] == ROUTE:
                shared[kind].append(None)
                cuts[kind].append([])
            elif step[0] == COMPUTE:
                pieces = [(step[i], step[i + 1]) for i in range(1, len(step), 2)]
                for part, place in pieces:
                    cuts[kind][-1].append((sibling_x(part, place).wait_recv,))
                    if place not in seen[kind]:
                        seen[kind].add(place)
                        cuts[kind][-1].append((columns_of, place))
                shared[kind].append(
                    [place * (rows // GRAIN) + STARTS[part] + i for part, place in pieces for i in range(SPLIT[part])]
                )
                cuts[kind].append([(sibling_y(part, place).start,) for part, place in pieces])
            else:
                cuts[kind][-1].append(({ARRIVE: arrive, REDUCE: reduce, SEND: send}[step[0]], kind, *step[1:]))

    def section(index):
        def body(kind):
            for action, *details in cuts[kind][index]:
                action(*details)

        by_kind(body)

    def finish(kind):
        for link, device in enumerate(neighbours[kind]):
            sent = sum(
                SPLIT[part]
                for place in range(2 * DEPTH)
                for part in range(PARTS)
                if link in onward(kind, part, place)
            )
            slot = xg.at[0, pl.ds(0, sent)]
            remote(slot, slot, ag_s.at[link], ag_r.at[0], device).wait_send()
            sent = sum(link in onward(kind, PARTS, place) for place in range(2 * DEPTH))
            if sent:
                slot = routes.at[0, pl.ds(0, sent)]
                remote(slot, slot, rt_s.at[link], rt_r.at[0], device).wait_send()
        remote(xg.at[0], xg.at[1], sx_s.at[0], sx_r.at[0], sibling).wait_send()
        remote(yb.at[1], ys, sy_s.at[0], sy_r.at[0], sibling).wait_send()
        remote(routes.at[0], routes.at[1], rx_s.at[0], rx_r.at[0], sibling).wait_send()
        returned = pl.ds(rows // GRAIN, (2 * DEPTH - 1) * (rows // GRAIN))
        remote(yb.at[0, returned], ys.at[returned], rs_s.at[0], rs_r.at[0, 0], sibling).wait_send()

    by_kind(greet)
    small = [
        pltpu.make_async_copy(src, dst, in_sem.at[PARTS + i])
        for i, (src, dst) in enumerate(((gain_hbm, gain_ref), (router_hbm, router_ref), (ids_hbm, ids_ref)))
    ]
    small[0].start()
    for part in range(PARTS):
        in_copy(part).start()
    for copy in small[1:]:
        copy.start()
    loads = [
        pltpu.make_async_copy(src.at[0], dst, load_sem.at[i])
        for i, (src, dst) in enumerate(((gate_hbm, gate_w), (up_hbm, up_w), (down_hbm, down_w)))
    ]
    for load in loads:
        load.start()
    small[0].wait()
    first = True
    for index, (corner, middle) in enumerate(zip(*shared)):
        section(index)
        if corner is None:
            for copy in small[1:]:
                copy.wait()
            route()
        else:
            if first:
                first = False
                for load in loads:
                    load.wait()
            compute(corner, middle)
    section(len(shared[0]))
    by_kind(finish)


def grid_local(hidden_in, norm_gain, router_weight, expert_ids, w_gate, w_up, w_down):
    rows, width = hidden_in.shape
    ff = w_gate.shape[2]
    count = router_weight.shape[1]
    places = 2 * DEPTH
    total = places * rows // GRAIN
    hbm = pl.BlockSpec(memory_space=pl.ANY)
    dma = pltpu.SemaphoreType.DMA
    pieces = places * PARTS
    return pl.pallas_call(
        grid_kernel,
        out_shape=pltpu.VMEM((rows, width), jnp.bfloat16),
        in_specs=[hbm] * 7,
        out_specs=pl.BlockSpec(memory_space=pltpu.VMEM),
        scratch_shapes=[
            pltpu.VMEM((rows, width), jnp.bfloat16),
            pltpu.VMEM((1, width), jnp.float32),
            pltpu.VMEM((count, width), jnp.bfloat16),
            pltpu.VMEM(expert_ids.shape[::-1], jnp.int32),
            pltpu.VMEM((width, ff), jnp.bfloat16),
            pltpu.VMEM((width, ff), jnp.bfloat16),
            pltpu.VMEM((ff, width), jnp.bfloat16),
            pltpu.VMEM((2, total, GRAIN, width), jnp.bfloat16),
            pltpu.VMEM((2, total, GRAIN, width), jnp.bfloat16),
            pltpu.VMEM((total, GRAIN, width), jnp.bfloat16),
            pltpu.VMEM((3, total, GRAIN, width), jnp.bfloat16),
            pltpu.VMEM((2 * GROUP * GRAIN, ff), jnp.bfloat16),
            pltpu.VMEM((2, places, count, rows), jnp.float32),
            pltpu.VMEM((2, total, GRAIN, rows), jnp.float32),
            dma((PARTS + 3,)), dma((3,)), dma((3,)), dma((pieces,)), dma((1,)), dma((pieces,)),
            dma((1,)), dma((pieces,)), dma((1,)), dma((3, pieces)),
            dma((3,)), dma((places,)), dma((1,)), dma((places,)),
        ],
        compiler_params=pltpu.CompilerParams(
            collective_id=0, has_side_effects=True, vmem_limit_bytes=56 * 1024 * 1024
        ),
    )(hidden_in, norm_gain.reshape(1, width), router_weight.T, expert_ids.T, w_gate, w_up, w_down)


def local(hidden_in, norm_gain, router_weight, expert_ids, w_gate, w_up, w_down):
    tok_rows, width = hidden_in.shape
    top_count = expert_ids.shape[1]
    num_experts = router_weight.shape[1]
    dev_count = lax.axis_size("expert")
    local_experts = w_gate.shape[0]
    cap_rows = tok_rows * top_count * 3 // (2 * num_experts)
    as_float = hidden_in.astype(jnp.float32)
    inv_rms = lax.rsqrt(jnp.mean(as_float * as_float, axis=1, keepdims=True) + 1e-06)
    normed = (as_float * inv_rms * norm_gain).astype(jnp.bfloat16)
    logits = jnp.dot(normed, router_weight, preferred_element_type=jnp.float32)
    expert_iota = jnp.arange(num_experts, dtype=jnp.int32)
    chosen = jnp.any(expert_ids[:, :, None] == expert_iota[None, None, :], axis=1)
    picked = jnp.where(chosen, jnp.exp(logits), 0.0)
    route_w = picked / jnp.sum(picked, axis=1, keepdims=True)
    earlier = jnp.arange(tok_rows)[:, None] > jnp.arange(tok_rows)[None, :]
    slot_index = jnp.dot(
        earlier.astype(jnp.float32), chosen.astype(jnp.float32), precision=lax.Precision.HIGHEST
    ).astype(jnp.int32)
    dispatch = chosen[:, :, None] & (slot_index[:, :, None] == jnp.arange(cap_rows)[None, None, :])
    outgoing = jnp.einsum(
        "tes,td->esd", dispatch.astype(jnp.bfloat16), normed, preferred_element_type=jnp.float32
    ).astype(jnp.bfloat16)
    arrived = lax.all_to_all(
        outgoing.reshape(dev_count, local_experts, cap_rows, width), "expert", 0, 0, tiled=True
    )
    gate_act = jnp.einsum("semd,edf->semf", arrived, w_gate, preferred_element_type=jnp.float32)
    up_act = jnp.einsum("semd,edf->semf", arrived, w_up, preferred_element_type=jnp.float32)
    hidden = (jax.nn.silu(gate_act) * up_act).astype(jnp.bfloat16)
    expert_out = jnp.einsum("semf,efd->semd", hidden, w_down, preferred_element_type=jnp.float32)
    returned = lax.all_to_all(expert_out.astype(jnp.bfloat16), "expert", 0, 0, tiled=True)
    combined = jnp.einsum(
        "tes,esd->td",
        jnp.where(dispatch, route_w[:, :, None], 0.0),
        returned.reshape(num_experts, cap_rows, width).astype(jnp.float32),
        precision=lax.Precision.HIGHEST,
    )
    return combined.astype(jnp.bfloat16)


def solution(mesh):
    in_specs = (
        P(("groups", "expert"), None),
        P(),
        P(),
        P(("groups", "expert"), None),
        P("expert", None, None),
        P("expert", None, None),
        P("expert", None, None),
    )
    out_specs = P(("groups", "expert"), None)
    gridded = mesh.shape["expert"] == 4 * DEPTH
    body = grid_local if gridded else local
    return jax.shard_map(body, mesh=mesh, in_specs=in_specs, out_specs=out_specs, check_vma=False)
```

```python
import jax
import jax.numpy as jnp
from jax import lax
from jax.experimental import pallas as pl
from jax.experimental.pallas import tpu as pltpu
from jax.sharding import PartitionSpec as P

DEPTH = 4
GRAIN = 16
GROUP = 4
INWARD, ACROSS, OUTWARD = range(3)
ARRIVE, REDUCE, COMPUTE, ROUTE, SEND = range(5)

SPLIT = (2, 2, 1, 2, 1)
ACROSS_LAST = (
    (True, True, True, False, False, False),
    (True, True, True, False, False, False),
)
STEPS = (
    (
        (3,), (0, 5, 0), (0, 3, 0), (4, 1, 3, 0), (0, 0, 0), (4, 0, 0, 0), (4, 1, 0, 0), (0, 4, 0),
        (4, 0, 4, 0), (0, 2, 0), (4, 1, 2, 0), (4, 0, 2, 0), (0, 1, 0), (4, 0, 1, 0), (0, 5, 1), (0, 5, 2),
        (2, 3, 0, 0, 0), (2, 2, 0, 4, 0, 1, 0), (0, 3, 1), (4, 1, 1, 0), (0, 1, 2), (4, 1, 1, 2), (4, 0, 3, 1), (0, 0, 1),
        (2, 1, 2, 3, 1), (0, 5, 3), (0, 2, 1), (0, 3, 2), (0, 4, 2), (0, 5, 4), (4, 1, 4, 0), (4, 0, 3, 0),
        (2, 0, 1, 3, 2), (0, 3, 4), (0, 1, 1), (1, 0, 1), (2, 3, 4, 1, 1), (0, 1, 4), (0, 1, 3), (0, 5, 6),
        (0, 4, 1), (4, 0, 4, 1), (1, 3, 2), (1, 1, 1), (2, 1, 3, 1, 4), (0, 4, 4), (1, 3, 4), (4, 1, 1, 4),
        (1, 1, 3), (2, 4, 4, 4, 1, 4, 2, 2, 1), (0, 5, 5), (0, 0, 6), (4, 1, 0, 6), (1, 4, 4), (1, 4, 2), (0, 3, 3),
        (0, 5, 7), (2, 3, 3, 0, 6), (1, 2, 1), (0, 2, 6), (4, 1, 2, 6), (0, 4, 6), (0, 1, 5), (1, 3, 3),
        (1, 1, 2), (2, 4, 6, 2, 6, 1, 5), (0, 3, 5), (0, 0, 7), (1, 4, 6), (1, 1, 5), (2, 3, 5, 0, 7), (0, 1, 6),
        (0, 2, 7), (4, 1, 1, 6), (1, 3, 5), (1, 0, 7), (0, 3, 6), (1, 1, 4), (0, 4, 3), (2, 3, 6, 2, 7, 4, 3),
        (0, 1, 7), (0, 2, 2), (4, 1, 2, 2), (1, 2, 7), (1, 3, 6), (2, 1, 7, 1, 6), (1, 4, 3), (1, 0, 6),
        (0, 4, 7), (0, 3, 7), (1, 1, 7), (0, 2, 3), (2, 4, 7, 2, 2, 3, 7), (0, 4, 5), (1, 2, 6), (1, 4, 7),
        (1, 3, 7), (0, 0, 4), (4, 1, 0, 4), (2, 2, 3, 4, 5, 0, 4), (1, 1, 6), (0, 2, 4), (4, 1, 2, 4), (1, 2, 3),
        (0, 0, 5), (1, 4, 5), (0, 2, 5), (0, 0, 2), (4, 1, 0, 2), (2, 2, 5, 0, 5, 2, 4), (1, 2, 2), (1, 2, 5),
        (1, 0, 5), (0, 0, 3), (2, 0, 3, 0, 2), (1, 0, 0), (1, 2, 4), (1, 2, 0), (1, 0, 3), (1, 0, 4),
        (1, 4, 1), (1, 0, 2), (1, 3, 1), (1, 4, 0), (1, 1, 0), (1, 3, 0),
    ),
    (
        (0, 0, 0), (3,), (0, 5, 0), (0, 2, 0), (0, 1, 0), (4, 2, 1, 0), (4, 1, 0, 0), (0, 3, 0),
        (4, 2, 3, 0), (4, 1, 3, 0), (4, 0, 3, 0), (4, 0, 1, 0), (0, 4, 0), (4, 2, 4, 0), (4, 1, 4, 0), (0, 5, 1),
        (0, 5, 2), (0, 5, 6), (4, 0, 4, 0), (2, 3, 0, 4, 0, 2, 0), (0, 0, 6), (4, 0, 0, 6), (0, 0, 1), (4, 1, 0, 6),
        (0, 3, 2), (4, 2, 3, 2), (2, 1, 0, 0, 0), (2, 3, 2, 0, 1), (0, 2, 6), (4, 1, 2, 6), (0, 1, 2), (4, 2, 1, 2),
        (4, 0, 2, 6), (4, 1, 1, 2), (0, 5, 4), (0, 4, 2), (4, 2, 4, 2), (1, 0, 1), (0, 4, 6), (4, 0, 4, 6),
        (0, 1, 6), (4, 0, 1, 6), (2, 1, 2, 2, 6, 4, 2), (0, 0, 4), (4, 1, 0, 4), (0, 2, 7), (4, 2, 0, 4), (0, 3, 7),
        (0, 0, 7), (0, 5, 7), (0, 5, 3), (0, 3, 1), (4, 0, 3, 1), (4, 2, 3, 1), (0, 4, 1), (0, 2, 4),
        (2, 2, 7, 0, 7, 4, 6), (0, 3, 6), (4, 0, 4, 1), (0, 1, 3), (2, 0, 4, 4, 1, 2, 4), (2, 3, 6, 1, 3), (0, 5, 5), (1, 0, 7),
        (4, 2, 2, 4), (4, 0, 3, 6), (0, 4, 4), (4, 2, 4, 4), (1, 1, 3), (0, 3, 3), (0, 0, 5), (0, 1, 4),
        (4, 2, 3, 3), (2, 3, 7, 0, 6), (4, 2, 1, 4), (4, 1, 1, 4), (1, 3, 2), (4, 0, 3, 7), (4, 1, 2, 4), (2, 0, 5, 3, 1),
        (0, 3, 4), (4, 2, 3, 4), (1, 2, 7), (2, 1, 4, 1, 6), (4, 2, 4, 1), (1, 0, 5), (0, 4, 7), (4, 0, 4, 7),
        (4, 0, 0, 0), (0, 4, 3), (4, 0, 2, 0), (4, 2, 2, 0), (2, 3, 4, 4, 7, 4, 4), (0, 3, 5), (4, 2, 3, 5), (0, 2, 5),
        (4, 1, 1, 6), (1, 4, 2), (0, 1, 5), (2, 2, 5, 3, 5, 4, 3), (2, 1, 5, 3, 3), (1, 2, 5), (0, 0, 2), (4, 1, 0, 2),
        (0, 4, 5), (4, 2, 4, 5), (1, 4, 4), (4, 2, 4, 3), (4, 2, 0, 2), (1, 1, 5), (1, 3, 3), (0, 2, 2),
        (2, 2, 2, 0, 2, 4, 5), (4, 2, 2, 2), (4, 1, 2, 2), (0, 1, 7), (1, 1, 2), (1, 4, 6), (4, 1, 2, 0), (4, 2, 0, 0),
        (1, 3, 1), (0, 0, 3), (1, 3, 4), (2, 1, 7, 0, 3), (4, 1, 1, 0), (0, 2, 3), (1, 0, 4), (1, 3, 6),
        (1, 0, 3), (1, 2, 4), (0, 2, 1), (1, 4, 5), (1, 1, 7), (1, 0, 6), (1, 3, 0), (1, 2, 6),
        (1, 3, 5), (1, 4, 7), (0, 1, 1), (2, 2, 1, 2, 3, 1, 1), (1, 3, 7), (1, 1, 4), (1, 4, 3), (1, 2, 3),
        (1, 2, 1), (1, 1, 1), (1, 1, 6), (1, 2, 2), (1, 4, 1), (1, 0, 2), (1, 2, 0), (1, 1, 0),
        (1, 4, 0), (1, 0, 0),
    ),
)

PARTS = len(SPLIT)
STARTS = tuple(sum(SPLIT[:part]) for part in range(PARTS))


def place_of(dz, dy):
    return dz % DEPTH * 2 + dy


def spot_of(kind, place):
    dz, dy = place // 2, place % 2
    return (dz - DEPTH if kind == 1 and dz == DEPTH - 1 else dz), dy


def along_z(kind):
    return {1: INWARD} if kind == 0 else {1: INWARD, -1: OUTWARD}


def across_last(kind, part, place):
    dz, _ = spot_of(kind, place)
    near = dz in (0, DEPTH - 1) if kind == 0 else dz in (0, 1)
    return ACROSS_LAST[kind if near else 1 - kind][part]


def onward(kind, part, place):
    dz, dy = spot_of(kind, place)
    links = along_z(kind)
    ways = (1, -1) if dz == 0 else ((-1,) if dz > 0 else (1,))
    depth_links = [links[way] for way in ways if way in links]
    if across_last(kind, part, place):
        return depth_links + [ACROSS] if dy == 0 else []
    return ([ACROSS] if dz == 0 and dy == 0 else []) + depth_links


def back(kind, part, place):
    dz, dy = spot_of(kind, place)
    if dy == 1 and (across_last(kind, part, place) or dz == 0):
        return ACROSS
    return along_z(kind)[1 if dz > 0 else -1]


def beyond(kind, link, place):
    dz, dy = spot_of(kind, place)
    if link == ACROSS:
        return kind, place_of(dz, 1 - dy), ACROSS
    if kind == 0:
        return 1, place_of(dz - 1, dy), OUTWARD
    if link == INWARD:
        return 1, place_of(1 - dz, dy), INWARD
    return 0, place_of(dz + 1, dy), INWARD


def grid_kernel(
    x_hbm, gain_hbm, router_hbm, ids_hbm, gate_hbm, up_hbm, down_hbm, out_ref,
    x_ref, gain_ref, router_ref, ids_ref, gate_w, up_w, down_w, xg, yb, ys, arrived, hb, routes, route_col,
    in_sem, load_sem, ag_s, ag_r, sx_s, sx_r, sy_s, sy_r, rs_s, rs_r, rt_s, rt_r, rx_s, rx_r,
):
    rows, width = x_ref.shape
    me = lax.axis_index("expert")
    core = me % 2
    y_at = (me // 2) % 2
    z_at = me // 4
    is_corner = z_at % 3 == 0
    sibling = me + 1 - 2 * core

    def device_at(z, y):
        return (z * 2 + y) * 2 + core

    across = device_at(z_at, 1 - y_at)
    neighbours = (
        (device_at(1 + z_at // 3, y_at), across),
        (device_at(3 - z_at, y_at), across, device_at(3 * (z_at - 1), y_at)),
    )

    def by_kind(body):
        for kind in range(2):
            pl.when(is_corner if kind == 0 else jnp.logical_not(is_corner))(lambda kind=kind: body(kind))

    def greet(kind):
        for device in neighbours[kind] + (sibling,):
            pl.semaphore_signal(
                barrier, inc=1, device_id={"expert": device}, device_id_type=pl.DeviceIdType.MESH
            )

    def remote(src, dst, send, recv, device):
        return pltpu.make_async_remote_copy(
            src_ref=src, dst_ref=dst, send_sem=send, recv_sem=recv,
            device_id={"expert": device}, device_id_type=pl.DeviceIdType.MESH,
        )

    def grains(part, place):
        return pl.ds(place * (rows // GRAIN) + STARTS[part], SPLIT[part])

    def number(part, place):
        return place * PARTS + part

    def gather_copy(kind, link, part, place):
        _, there, _ = beyond(kind, link, place)
        return remote(
            xg.at[0, grains(part, place)], xg.at[0, grains(part, there)],
            ag_s.at[link], ag_r.at[number(part, there)], neighbours[kind][link],
        )

    def gathered(part, place):
        at, slot = number(part, place), grains(part, place)
        return remote(xg.at[0, slot], xg.at[0, slot], ag_s.at[0], ag_r.at[at], sibling)

    def sibling_x(part, place):
        at, slot = number(part, place), grains(part, place)
        return remote(xg.at[0, slot], xg.at[1, slot], sx_s.at[0], sx_r.at[at], sibling)

    def sibling_y(part, place):
        at, slot = number(part, place), grains(part, place)
        return remote(yb.at[1, slot], ys.at[slot], sy_s.at[0], sy_r.at[at], sibling)

    def route_copy(kind, link, place):
        _, there, _ = beyond(kind, link, place)
        return remote(
            routes.at[0, place], routes.at[0, there], rt_s.at[link], rt_r.at[there],
            neighbours[kind][link],
        )

    def routed(place):
        return remote(routes.at[0, place], routes.at[0, place], rt_s.at[0], rt_r.at[place], sibling)

    def sibling_route(place):
        return remote(routes.at[0, place], routes.at[1, place], rx_s.at[0], rx_r.at[place], sibling)

    def reduce_copy(kind, part, place):
        link = back(kind, part, place)
        _, there, entry = beyond(kind, link, place)
        return remote(
            yb.at[0, grains(part, place)], arrived.at[entry, grains(part, there)],
            rs_s.at[0], rs_r.at[entry, number(part, there)], neighbours[kind][link],
        )

    def reduced(link, part, place):
        at, slot = number(part, place), grains(part, place)
        return remote(yb.at[0, slot], arrived.at[link, slot], rs_s.at[0], rs_r.at[link, at], sibling)

    def in_copy(part):
        part_rows = pl.ds(STARTS[part] * GRAIN, SPLIT[part] * GRAIN)
        return pltpu.make_async_copy(x_hbm.at[part_rows], x_ref.at[part_rows], in_sem.at[part])

    def norm(part):
        in_copy(part).wait()
        first, last = STARTS[part], STARTS[part] + SPLIT[part]
        as_float = x_ref[first * GRAIN : last * GRAIN].astype(jnp.float32)
        inv_rms = lax.rsqrt(jnp.mean(as_float * as_float, axis=1, keepdims=True) + 1e-06)
        normed = (as_float * inv_rms * gain_ref[...]).astype(jnp.bfloat16)
        xg[0, first:last] = normed.reshape(last - first, GRAIN, width)

    def arrive(kind, part, place):
        if part == PARTS:
            if place != 0:
                routed(place).wait_recv()
            for link in onward(kind, part, place):
                route_copy(kind, link, place).start()
            sibling_route(place).start()
            return
        if place != 0:
            gathered(part, place).wait_recv()
        sibling_x(part, place).start()

    def send(kind, link, part, place):
        gather_copy(kind, link, part, place).start()

    def reduce(kind, part, place):
        sibling_y(part, place).wait_recv()
        links = onward(kind, part, place)
        for link in links:
            reduced(link, part, place).wait_recv()
        for grain in range(SPLIT[part]):
            at = place * (rows // GRAIN) + STARTS[part] + grain
            value = yb[0, at].astype(jnp.float32) + ys[at].astype(jnp.float32)
            for link in links:
                value = value + arrived[link, at].astype(jnp.float32)
            value = value.astype(jnp.bfloat16)
            if place == 0:
                first = (STARTS[part] + grain) * GRAIN
                out_ref[first : first + GRAIN] = value
            else:
                yb[0, at] = value
        if place != 0:
            reduce_copy(kind, part, place).start()

    diagonal = lax.broadcasted_iota(jnp.int32, (rows, rows), 0) == lax.broadcasted_iota(
        jnp.int32, (rows, rows), 1
    )

    def columns_of(place):
        sibling_route(place).wait_recv()
        for lane in range(2):
            values = routes[lane, place, pl.ds(me, 1), :]
            column = jnp.sum(jnp.where(diagonal, values, 0.0), axis=1, keepdims=True)
            spread = jnp.broadcast_to(column, (rows, rows))
            for grain in range(rows // GRAIN):
                at = place * (rows // GRAIN) + grain
                route_col[lane, at] = spread[grain * GRAIN : (grain + 1) * GRAIN]

    def route():
        logits = lax.dot_general(
            router_ref[...], xg[0, : rows // GRAIN].reshape(rows, width), (((1,), (1,)), ((), ())),
            preferred_element_type=jnp.float32,
        )
        exp_logits = jnp.exp(logits)
        expert_iota = lax.broadcasted_iota(jnp.int32, logits.shape, 0)
        chosen = expert_iota < 0
        for k in range(ids_ref.shape[0]):
            chosen = chosen | (ids_ref[k : k + 1, :] == expert_iota)
        picked = jnp.where(chosen, exp_logits, 0.0)
        routes[0, 0] = picked / jnp.sum(picked, axis=0, keepdims=True)

    def compute(corner_grains, middle_grains):
        at = [jnp.where(is_corner, a, b) for a, b in zip(corner_grains, middle_grains)]
        x = jnp.concatenate([xg[lane, a] for lane in range(2) for a in at], axis=0)
        gate = jnp.dot(x, gate_w[...], preferred_element_type=jnp.float32)
        up = jnp.dot(x, up_w[...], preferred_element_type=jnp.float32)
        hb[...] = (gate / (1.0 + jnp.exp(-gate)) * up).astype(jnp.bfloat16)
        y = jnp.dot(hb[...], down_w[...], preferred_element_type=jnp.float32)
        for lane in range(2):
            for i, a in enumerate(at):
                first = (lane * GROUP + i) * GRAIN
                weight = jnp.concatenate([route_col[lane, a]] * (width // rows), axis=1)
                yb[lane, a] = (y[first : first + GRAIN] * weight).astype(jnp.bfloat16)

    barrier = pltpu.get_barrier_semaphore()

    cuts = [[[]], [[]]]
    shared = [[], []]
    seen = [set(), set()]
    for kind in range(2):
        normed, greeted = set(), False
        for step in STEPS[kind]:
            own = step[1:2] if step[0] == ARRIVE and step[2] == 0 else ()
            for part in range(PARTS) if step[0] == ROUTE else own:
                if part < PARTS and part not in normed:
                    normed.add(part)
                    cuts[kind][-1].append((norm, part))
            if not greeted:
                greeted = True
                cuts[kind][-1].append((pl.semaphore_wait, barrier, len(neighbours[kind]) + 1))
            if step[0] == ROUTE:
                shared[kind].append(None)
                cuts[kind].append([])
            elif step[0] == COMPUTE:
                pieces = [(step[i], step[i + 1]) for i in range(1, len(step), 2)]
                for part, place in pieces:
                    cuts[kind][-1].append((sibling_x(part, place).wait_recv,))
                    if place not in seen[kind]:
                        seen[kind].add(place)
                        cuts[kind][-1].append((columns_of, place))
                shared[kind].append(
                    [place * (rows // GRAIN) + STARTS[part] + i for part, place in pieces for i in range(SPLIT[part])]
                )
                cuts[kind].append([(sibling_y(part, place).start,) for part, place in pieces])
            else:
                cuts[kind][-1].append(({ARRIVE: arrive, REDUCE: reduce, SEND: send}[step[0]], kind, *step[1:]))

    def section(index):
        def body(kind):
            for action, *details in cuts[kind][index]:
                action(*details)

        by_kind(body)

    def finish(kind):
        for link, device in enumerate(neighbours[kind]):
            sent = sum(
                SPLIT[part]
                for place in range(2 * DEPTH)
                for part in range(PARTS)
                if link in onward(kind, part, place)
            )
            slot = xg.at[0, pl.ds(0, sent)]
            remote(slot, slot, ag_s.at[link], ag_r.at[0], device).wait_send()
            sent = sum(link in onward(kind, PARTS, place) for place in range(2 * DEPTH))
            if sent:
                slot = routes.at[0, pl.ds(0, sent)]
                remote(slot, slot, rt_s.at[link], rt_r.at[0], device).wait_send()
        remote(xg.at[0], xg.at[1], sx_s.at[0], sx_r.at[0], sibling).wait_send()
        remote(yb.at[1], ys, sy_s.at[0], sy_r.at[0], sibling).wait_send()
        remote(routes.at[0], routes.at[1], rx_s.at[0], rx_r.at[0], sibling).wait_send()
        returned = pl.ds(rows // GRAIN, (2 * DEPTH - 1) * (rows // GRAIN))
        remote(yb.at[0, returned], ys.at[returned], rs_s.at[0], rs_r.at[0, 0], sibling).wait_send()

    by_kind(greet)
    small = [
        pltpu.make_async_copy(src, dst, in_sem.at[PARTS + i])
        for i, (src, dst) in enumerate(((gain_hbm, gain_ref), (router_hbm, router_ref), (ids_hbm, ids_ref)))
    ]
    small[0].start()
    for part in range(PARTS):
        in_copy(part).start()
    for copy in small[1:]:
        copy.start()
    loads = [
        pltpu.make_async_copy(src.at[0], dst, load_sem.at[i])
        for i, (src, dst) in enumerate(((gate_hbm, gate_w), (up_hbm, up_w), (down_hbm, down_w)))
    ]
    for load in loads:
        load.start()
    small[0].wait()
    first = True
    for index, (corner, middle) in enumerate(zip(*shared)):
        section(index)
        if corner is None:
            for copy in small[1:]:
                copy.wait()
            route()
        else:
            if first:
                first = False
                for load in loads:
                    load.wait()
            compute(corner, middle)
    section(len(shared[0]))
    by_kind(finish)


def grid_local(hidden_in, norm_gain, router_weight, expert_ids, w_gate, w_up, w_down):
    rows, width = hidden_in.shape
    ff = w_gate.shape[2]
    count = router_weight.shape[1]
    places = 2 * DEPTH
    total = places * rows // GRAIN
    hbm = pl.BlockSpec(memory_space=pl.ANY)
    dma = pltpu.SemaphoreType.DMA
    pieces = places * PARTS
    return pl.pallas_call(
        grid_kernel,
        out_shape=pltpu.VMEM((rows, width), jnp.bfloat16),
        in_specs=[hbm] * 7,
        out_specs=pl.BlockSpec(memory_space=pltpu.VMEM),
        scratch_shapes=[
            pltpu.VMEM((rows, width), jnp.bfloat16),
            pltpu.VMEM((1, width), jnp.float32),
            pltpu.VMEM((count, width), jnp.bfloat16),
            pltpu.VMEM(expert_ids.shape[::-1], jnp.int32),
            pltpu.VMEM((width, ff), jnp.bfloat16),
            pltpu.VMEM((width, ff), jnp.bfloat16),
            pltpu.VMEM((ff, width), jnp.bfloat16),
            pltpu.VMEM((2, total, GRAIN, width), jnp.bfloat16),
            pltpu.VMEM((2, total, GRAIN, width), jnp.bfloat16),
            pltpu.VMEM((total, GRAIN, width), jnp.bfloat16),
            pltpu.VMEM((3, total, GRAIN, width), jnp.bfloat16),
            pltpu.VMEM((2 * GROUP * GRAIN, ff), jnp.bfloat16),
            pltpu.VMEM((2, places, count, rows), jnp.float32),
            pltpu.VMEM((2, total, GRAIN, rows), jnp.float32),
            dma((PARTS + 3,)), dma((3,)), dma((3,)), dma((pieces,)), dma((1,)), dma((pieces,)),
            dma((1,)), dma((pieces,)), dma((1,)), dma((3, pieces)),
            dma((3,)), dma((places,)), dma((1,)), dma((places,)),
        ],
        compiler_params=pltpu.CompilerParams(
            collective_id=0, has_side_effects=True, vmem_limit_bytes=56 * 1024 * 1024
        ),
    )(hidden_in, norm_gain.reshape(1, width), router_weight.T, expert_ids.T, w_gate, w_up, w_down)


def local(hidden_in, norm_gain, router_weight, expert_ids, w_gate, w_up, w_down):
    tok_rows, width = hidden_in.shape
    top_count = expert_ids.shape[1]
    num_experts = router_weight.shape[1]
    dev_count = lax.axis_size("expert")
    local_experts = w_gate.shape[0]
    cap_rows = tok_rows * top_count * 3 // (2 * num_experts)
    as_float = hidden_in.astype(jnp.float32)
    inv_rms = lax.rsqrt(jnp.mean(as_float * as_float, axis=1, keepdims=True) + 1e-06)
    normed = (as_float * inv_rms * norm_gain).astype(jnp.bfloat16)
    logits = jnp.dot(normed, router_weight, preferred_element_type=jnp.float32)
    expert_iota = jnp.arange(num_experts, dtype=jnp.int32)
    chosen = jnp.any(expert_ids[:, :, None] == expert_iota[None, None, :], axis=1)
    picked = jnp.where(chosen, jnp.exp(logits), 0.0)
    route_w = picked / jnp.sum(picked, axis=1, keepdims=True)
    earlier = jnp.arange(tok_rows)[:, None] > jnp.arange(tok_rows)[None, :]
    slot_index = jnp.dot(
        earlier.astype(jnp.float32), chosen.astype(jnp.float32), precision=lax.Precision.HIGHEST
    ).astype(jnp.int32)
    dispatch = chosen[:, :, None] & (slot_index[:, :, None] == jnp.arange(cap_rows)[None, None, :])
    outgoing = jnp.einsum(
        "tes,td->esd", dispatch.astype(jnp.bfloat16), normed, preferred_element_type=jnp.float32
    ).astype(jnp.bfloat16)
    arrived = lax.all_to_all(
        outgoing.reshape(dev_count, local_experts, cap_rows, width), "expert", 0, 0, tiled=True
    )
    gate_act = jnp.einsum("semd,edf->semf", arrived, w_gate, preferred_element_type=jnp.float32)
    up_act = jnp.einsum("semd,edf->semf", arrived, w_up, preferred_element_type=jnp.float32)
    hidden = (jax.nn.silu(gate_act) * up_act).astype(jnp.bfloat16)
    expert_out = jnp.einsum("semf,efd->semd", hidden, w_down, preferred_element_type=jnp.float32)
    returned = lax.all_to_all(expert_out.astype(jnp.bfloat16), "expert", 0, 0, tiled=True)
    combined = jnp.einsum(
        "tes,esd->td",
        jnp.where(dispatch, route_w[:, :, None], 0.0),
        returned.reshape(num_experts, cap_rows, width).astype(jnp.float32),
        precision=lax.Precision.HIGHEST,
    )
    return combined.astype(jnp.bfloat16)


def solution(mesh):
    in_specs = (
        P(("groups", "expert"), None),
        P(),
        P(),
        P(("groups", "expert"), None),
        P("expert", None, None),
        P("expert", None, None),
        P("expert", None, None),
    )
    out_specs = P(("groups", "expert"), None)
    gridded = mesh.shape["expert"] == 4 * DEPTH
    body = grid_local if gridded else local
    return jax.shard_map(body, mesh=mesh, in_specs=in_specs, out_specs=out_specs, check_vma=False)
```
